128 devices in a mesh: region: 4 (over x), block: 32 (over z, y, core).
Axes of the slice: x: 4, y: 4, z: 4, core: 2. Of those that a mesh axis runs over, the one named last changes fastest.
Arguments:
- env_left: float32 [4, 17, 32, 128, 128], P('region', None, 'block'), may hold values from -6 to 6
- env_right: float32 [4, 17, 32, 128, 128], P('region', None, 'block'), may hold values from -0.125 to 0.125
- site_tensors: float32 [4, 2, 4, 32, 128, 128], P('region', None, None, 'block'), may hold values from -0.5 to 0.5
- pair_state: float32 [4, 16, 32, 128, 128], P('region', None, 'block'), may hold values from -0.5 to 0.5
- mpo_sites: float32 [4, 2, 17, 17, 4, 4], P('region'), may hold values from -0.75 to 0.75
- mpo_pair: float32 [4, 2, 17, 17, 4, 4], P('region'), may hold values from -0.75 to 0.75
- channel_class: int32 [17], replicated, may hold values from 0 to 4, as said below
- live_rows: int32 [4, 3, 32], P('region'), may hold values from 64 to 128, as said below
- region_sites: int32 [4], P('region'), may hold values from 1 to 2, as said below
Outputs:
- new_env: float32 [4, 17, 32, 128, 128], P('region', None, 'block')
- pair_image: float32 [4, 16, 32, 128, 128], P('region', None, 'block')
The draws below stay inside these ranges and needn't reach their ends.
Inputs may be any that keep to these rules, and one draw needn't show every extreme that they name: `channel_class`: each of the five classes is taken by at least 3 channels. `live_rows`: every bond of every region has a sector with exactly 128 live states. `region_sites`: some region updates exactly 2 sites.
All inputs are finite; a program needn't handle non-finite values.
Results may differ from the reference program's by a relative error of at most 0.0001.
Values sent between devices are 32-bit elements; how exact they have to be, the bound alone decides.
No kernel may reach another device: no remote copies, remote signals or barrier semaphores. Data moves between devices by JAX's collectives and lax.ppermute only.
A program may use at most 192 MiB of HBM per device.

```python
import jax
import jax.numpy as jnp
from jax import lax

NSEC = 32
TILE = 128
NW = 17
ND = 8
MAXLEN = 2
REGIONS = 4


def draw_channel_class(key, part):
    classes = jnp.arange(NW, dtype=jnp.int32) % 5
    return jax.random.permutation(key, classes).astype(jnp.int32)


def draw_live_rows(key, part):
    first_key, second_key = jax.random.split(jax.random.fold_in(key, 11))
    counts = jax.random.randint(first_key, (REGIONS, MAXLEN + 1, NSEC), TILE // 2, TILE + 1)
    chosen = jax.random.randint(second_key, (REGIONS, MAXLEN + 1, 1), 0, NSEC)
    sector_ids = jnp.arange(NSEC, dtype=jnp.int32)[None, None, :]
    return jnp.where(sector_ids == chosen, TILE, counts).astype(jnp.int32)


def draw_region_sites(key, part):
    first_key, second_key = jax.random.split(jax.random.fold_in(key, 23))
    counts = jax.random.randint(first_key, (REGIONS,), 1, MAXLEN + 1)
    chosen = jax.random.randint(second_key, (), 0, REGIONS)
    return jnp.where(jnp.arange(REGIONS, dtype=jnp.int32) == chosen, MAXLEN, counts).astype(jnp.int32)


def steps_of(stream_key, shape, shards, smallest, high):
    gain = 1.0
    for position, shards_of in shards:
        steps = jax.random.uniform(jax.random.fold_in(jax.random.fold_in(stream_key, 6), position), (shards_of,), jnp.float32, smallest / len(shards), high / len(shards))
        gain = gain * jnp.repeat(jnp.exp(steps), shape[position] // shards_of).reshape((-1,) + (1,) * (len(shape) - 1 - position))
    return gain


def centred(key, shape, deviation, limit, pieces=(), kind=jnp.bfloat16):
    result = deviation * jax.random.normal(key, shape, jnp.float32)
    if pieces:
        result = result * steps_of(key, shape, pieces, -0.22, 0.18)
    return jnp.clip(result, -limit, limit).astype(kind)


def setup_inputs(seed: int = 0) -> dict:
    streams_of = jax.random.split(jax.random.key(seed), 10)
    return {
        "env_left": centred(streams_of[0], (REGIONS, NW, NSEC, TILE, TILE), 1.0, 6.0, ((0, 4), (2, 32)), jnp.float32),
        "env_right": centred(streams_of[1], (REGIONS, NW, NSEC, TILE, TILE), (TILE * NW) ** -0.5, 0.125, ((0, 4), (2, 32)), jnp.float32),
        "site_tensors": centred(streams_of[2], (REGIONS, MAXLEN, 4, NSEC, TILE, TILE), TILE ** -0.5, 0.5, ((0, 4), (3, 32)), jnp.float32),
        "pair_state": centred(streams_of[3], (REGIONS, 16, NSEC, TILE, TILE), TILE ** -0.5, 0.5, ((0, 4), (2, 32)), jnp.float32),
        "mpo_sites": centred(streams_of[4], (REGIONS, MAXLEN, NW, NW, 4, 4), (4 * NW) ** -0.5, 0.75, ((0, 4),), jnp.float32),
        "mpo_pair": centred(streams_of[5], (REGIONS, 2, NW, NW, 4, 4), (4 * NW) ** -0.5, 0.75, ((0, 4),), jnp.float32),
        "channel_class": draw_channel_class(jax.random.fold_in(streams_of[9], 71), 0),
        "live_rows": draw_live_rows(jax.random.fold_in(streams_of[9], 71), 0),
        "region_sites": draw_region_sites(jax.random.fold_in(streams_of[9], 71), 0),
    }


HIGHEST = lax.Precision.HIGHEST


def state_steps():
    return [0, ND, 1, ND + 1]


def class_steps():
    return [0, 1, -1, ND, -ND]


def pair_steps():
    single = state_steps()
    return [single[upper_state] + single[lower_state] for upper_state in range(4) for lower_state in range(4)]


def move_sectors(blocks, offset, sector_dim):
    extent = blocks.shape[sector_dim]
    rolled = jnp.roll(blocks, -offset, axis=sector_dim)
    target = jnp.arange(extent, dtype=jnp.int32) + offset
    inside = ((target >= 0) & (target < extent)).astype(blocks.dtype)
    layout = [1] * blocks.ndim
    layout[sector_dim] = extent
    return rolled * inside.reshape(layout)


def in_range(offsets):
    target = jnp.arange(NSEC, dtype=jnp.int32)[None, :] + offsets[:, None]
    return ((target >= 0) & (target < NSEC)).astype(jnp.float32)


def row_masks(live_count):
    return (jnp.arange(TILE, dtype=jnp.int32)[None, :] < live_count[:, None]).astype(jnp.float32)


def allowed_terms(shifts):
    single = jnp.array(state_steps(), dtype=jnp.int32)
    conserved = shifts[None, :, None, None] == shifts[:, None, None, None] + single[None, None, None, :] - single[None, None, :, None]
    return conserved.astype(jnp.float32)


def env_update(environment, tensor, mpo_site, channel_class, shifts, live_count):
    single = state_steps()
    shifted = jnp.stack([move_sectors(tensor, offset, 1) for offset in class_steps()])
    ket_blocks = jnp.take(shifted, channel_class, axis=0)
    product = jnp.einsum("wjab,wtjbc->wtjac", environment, ket_blocks, precision=HIGHEST)
    weights = mpo_site * allowed_terms(shifts)
    contracted = jnp.einsum("wxst,wtjac->xsjac", weights, product, precision=HIGHEST)
    closed = jnp.einsum("sjba,xsjbc->xsjac", tensor, contracted, precision=HIGHEST)
    summed = move_sectors(closed[:, 0], -single[0], 1)
    for local_state in range(1, 4):
        summed = summed + move_sectors(closed[:, local_state], -single[local_state], 1)
    row_mask = row_masks(live_count)
    columns = jnp.take(jnp.stack([move_sectors(row_mask, offset, 0) for offset in class_steps()]), channel_class, axis=0)
    return summed * row_mask[None, :, :, None] * columns[:, :, None, :]


def pair_update(boundary, pair_blocks, right_env, mpo_left, mpo_right, shifts, live_count):
    margin = 2 * ND + 2
    pair_pad = jnp.pad(pair_blocks, ((0, 0), (margin, margin), (0, 0), (0, 0)))
    right_pad = jnp.pad(right_env, ((0, 0), (margin, margin), (0, 0), (0, 0)))
    offsets_pair = jnp.array(pair_steps(), dtype=jnp.int32)
    row_mask = row_masks(live_count)
    mask_pad = jnp.pad(row_mask, ((margin, margin), (0, 0)))
    left_rule = mpo_left * allowed_terms(shifts)
    right_rule = mpo_right * allowed_terms(shifts)

    def one_sector(sector):
        left_block = lax.dynamic_index_in_dim(boundary, sector, 1, keepdims=False)
        ket_blocks = jnp.take(pair_pad, sector + margin + shifts, axis=1)
        product = jnp.einsum("wab,pwbc->wpac", left_block, ket_blocks, precision=HIGHEST)
        product = product.reshape(NW, 4, 4, TILE, TILE)
        middle = jnp.einsum("wxst,wtuac->xsuac", left_rule, product, precision=HIGHEST)
        outermost = jnp.einsum("wvst,wutac->vusac", right_rule, middle, precision=HIGHEST)
        outermost = outermost.reshape(NW, 16, TILE, TILE)
        right_blocks = jnp.take(right_pad, sector + margin + offsets_pair, axis=1)
        pair_part = jnp.einsum("vpac,vpbc->pab", outermost, right_blocks, precision=HIGHEST)
        row_keep = lax.dynamic_index_in_dim(row_mask, sector, 0, keepdims=False)
        col_keep = jnp.take(mask_pad, sector + margin + offsets_pair, axis=0)
        return pair_part * row_keep[None, :, None] * col_keep[:, None, :]

    images = lax.map(one_sector, jnp.arange(NSEC, dtype=jnp.int32))
    return jnp.moveaxis(images, 0, 1)


def reference(env_left, env_right, site_tensors, pair_state, mpo_sites, mpo_pair, channel_class, live_rows, region_sites):
    shifts = jnp.take(jnp.array(class_steps(), dtype=jnp.int32), channel_class)
    env_keep = in_range(shifts)[:, :, None, None]
    state_keep = in_range(jnp.array(state_steps(), dtype=jnp.int32))[:, :, None, None]
    pair_keep = in_range(jnp.array(pair_steps(), dtype=jnp.int32))[:, :, None, None]
    starts = []
    updated = []
    for region in range(REGIONS):
        environment = env_left[region] * env_keep
        starts.append(environment)
        for site_step in range(MAXLEN):
            tensor = site_tensors[region, site_step] * state_keep
            stepped = env_update(environment, tensor, mpo_sites[region, site_step], channel_class, shifts, live_rows[region, site_step])
            environment = jnp.where(site_step < region_sites[region], stepped, environment)
        updated.append(environment)
    images = []
    for region in range(REGIONS):
        boundary = starts[0] if region == 0 else updated[region - 1]
        images.append(pair_update(boundary, pair_state[region] * pair_keep, env_right[region] * env_keep, mpo_pair[region, 0], mpo_pair[region, 1], shifts, live_rows[region, MAXLEN]))
    return jnp.stack(updated), jnp.stack(images)
```

```python
import jax
import jax.numpy as jnp
from jax import lax
from jax.sharding import PartitionSpec as P

NSEC = 32
TILE = 128
NW = 17
ND = 8
MAXLEN = 2
STATE_STEPS = (0, ND, 1, ND + 1)
CLASS_STEPS = (0, 1, -1, ND, -ND)
PAIR_STEPS = tuple(a + b for a in STATE_STEPS for b in STATE_STEPS)
PRECISION = lax.Precision.HIGH


def fetch(blocks, offset, axis="block"):
    length = lax.axis_size(axis)
    pairs = [(i, i - offset) for i in range(length) if 0 <= i - offset < length]
    return lax.ppermute(blocks, axis, pairs)


def inside(sector, offsets):
    target = sector + jnp.array(offsets, dtype=jnp.int32)
    return ((target >= 0) & (target < NSEC)).astype(jnp.float32)


def allowed_terms(shifts):
    single = jnp.array(STATE_STEPS, dtype=jnp.int32)
    conserved = (
        shifts[None, :, None, None]
        == shifts[:, None, None, None] + single[None, None, None, :] - single[None, None, :, None]
    )
    return conserved.astype(jnp.float32)


def row_mask(live_count, sectors):
    valid = (sectors >= 0) & (sectors < NSEC)
    count = jnp.where(valid, jnp.take(live_count, jnp.clip(sectors, 0, NSEC - 1)), 0)
    return (jnp.arange(TILE, dtype=jnp.int32)[None, :] < count[:, None]).astype(jnp.float32)


def env_update(environment, kets, tensor, rule, channel_class, rows, columns):
    ket_blocks = jnp.take(kets, channel_class, axis=0)
    product = jnp.einsum("wab,wtbc->wtac", environment, ket_blocks, precision=PRECISION)
    contracted = jnp.einsum("wxst,wtac->sxac", rule, product, precision=PRECISION)
    closed = jnp.einsum("sba,sxbc->sxac", tensor, contracted, precision=PRECISION)
    below = fetch(closed[2:4], -1)
    partial = fetch(closed[1] + below[1], -ND)
    return (closed[0] + below[0] + partial) * rows[0][None, :, None] * columns[:, None, :]


def shards(
    env_left,
    env_right,
    site_tensors,
    pair_state,
    mpo_sites,
    mpo_pair,
    channel_class,
    live_rows,
    region_sites,
):
    sector = lax.axis_index("block")
    shifts = jnp.take(jnp.array(CLASS_STEPS, dtype=jnp.int32), channel_class)
    env_keep = ((sector + shifts >= 0) & (sector + shifts < NSEC)).astype(jnp.float32)
    env_keep = env_keep[:, None, None]
    start = env_left[0, :, 0] * env_keep
    tensors = site_tensors[0, :, :, 0] * inside(sector, STATE_STEPS)[None, :, None, None]
    pair_blocks = pair_state[0, :, 0] * inside(sector, PAIR_STEPS)[:, None, None]
    right = env_right[0, :, 0] * env_keep
    allowed = allowed_terms(shifts)

    kets = jnp.stack([tensors] + [fetch(tensors, offset) for offset in CLASS_STEPS[1:]])
    down = fetch(jnp.concatenate([pair_blocks, right]), ND)
    side = fetch(jnp.concatenate([pair_blocks, right]), 1)
    pair_kets = jnp.stack(
        [pair_blocks, side[:16], fetch(pair_blocks, -1), down[:16], fetch(pair_blocks, -ND)]
    )
    right_8 = down[16:]
    right_16 = fetch(right_8, ND)
    right_1 = side[16:]
    right_2 = fetch(right_1, 1)
    far_1 = fetch(jnp.concatenate([right_8, right_16]), 1)
    far_2 = fetch(far_1, 1)
    rights = {
        0: right,
        1: right_1,
        2: right_2,
        ND: right_8,
        2 * ND: right_16,
        ND + 1: far_1[:NW],
        2 * ND + 1: far_1[NW:],
        ND + 2: far_2[:NW],
        2 * ND + 2: far_2[NW:],
    }

    environment = start
    for site in range(MAXLEN):
        stepped = env_update(
            environment,
            kets[:, site],
            tensors[site],
            mpo_sites[0, site] * allowed,
            channel_class,
            row_mask(live_rows[0, site], sector[None]),
            row_mask(live_rows[0, site], sector + shifts),
        )
        environment = jnp.where(site < region_sites[0], stepped, environment)
    passed = fetch(environment, -1, "region")
    boundary = jnp.where(lax.axis_index("region") == 0, start, passed)

    ket_blocks = jnp.take(pair_kets, channel_class, axis=0)
    product = jnp.einsum("wab,wpbc->wpac", boundary, ket_blocks, precision=PRECISION)
    product = product.reshape(NW, 4, 4, TILE, TILE)
    middle = jnp.einsum("wxst,wtuac->xsuac", mpo_pair[0, 0] * allowed, product, precision=PRECISION)
    outer = jnp.einsum("wvst,wutac->usvac", mpo_pair[0, 1] * allowed, middle, precision=PRECISION)
    outer = outer.reshape(16, NW, TILE, TILE)
    images = jnp.stack(
        [
            jnp.einsum("vac,vbc->ab", outer[p], rights[step], precision=PRECISION)
            for p, step in enumerate(PAIR_STEPS)
        ]
    )
    rows = row_mask(live_rows[0, MAXLEN], sector[None])
    columns = row_mask(live_rows[0, MAXLEN], sector + jnp.array(PAIR_STEPS, dtype=jnp.int32))
    images = images * rows[0][None, :, None] * columns[:, None, :]
    return environment[None, :, None], images[None, :, None]


def solution(mesh):
    in_specs = (
        P("region", None, "block", None, None),
        P("region", None, "block", None, None),
        P("region", None, None, "block", None, None),
        P("region", None, "block", None, None),
        P("region", None, None, None, None, None),
        P("region", None, None, None, None, None),
        P(),
        P("region", None, None),
        P("region"),
    )
    out_specs = (P("region", None, "block", None, None), P("region", None, "block", None, None))
    return jax.shard_map(shards, mesh=mesh, in_specs=in_specs, out_specs=out_specs, check_vma=False)
```

```python
import functools
import jax
import jax.numpy as jnp
from jax import lax
from jax.experimental import pallas as pl
from jax.experimental.pallas import tpu as pltpu
from jax.sharding import PartitionSpec as P

NSEC = 32
TILE = 128
NW = 17
ND = 8
MAXLEN = 2
STATE_STEPS = (0, ND, 1, ND + 1)
CLASS_STEPS = (0, 1, -1, ND, -ND)
PAIR_STEPS = tuple(a + b for a in STATE_STEPS for b in STATE_STEPS)
NEEDED = (0, 1, 2, 8, 9, 10, 16, 17, 18)
LONG = 11
SHORT = 5
F32 = jnp.float32
BF16 = jnp.bfloat16


def mix_tables(channel_class, rules):
    steps = jnp.array(STATE_STEPS, dtype=jnp.int32)
    shifts = jnp.take(jnp.array(CLASS_STEPS, dtype=jnp.int32), channel_class)
    down = (jnp.arange(4) // 2)[:, None]
    up = (jnp.arange(4) % 2)[:, None]
    kind = channel_class[None, :]
    three = (
        (kind == 0)
        | ((kind == 1) & (down == 0))
        | ((kind == 2) & (down == 1))
        | ((kind == 3) & (up == 0))
        | ((kind == 4) & (up == 1))
    )
    key = jnp.where(three, 0, NW) + jnp.arange(NW, dtype=jnp.int32)[None, :]
    place = (key[:, None, :] < key[:, :, None]).sum(-1)
    hot = place[:, None, :] == jnp.arange(NW, dtype=jnp.int32)[None, :, None]
    out = jnp.where(hot, jnp.arange(NW, dtype=jnp.int32), 0).sum(-1).astype(jnp.int32)
    goal = jnp.where(hot, shifts, 0).sum(-1)
    source = (shifts[:, None] + steps[None, :]).reshape(-1)
    allowed = (goal + steps[:, None])[:, :, None] == source[None, None, :]
    size = 4 * NW
    before = (jnp.arange(size)[:, None] < jnp.arange(size)[None, :]).astype(F32)
    rank = jnp.einsum("sim,mn->sin", allowed.astype(F32), before).astype(jnp.int32)
    term = allowed[..., None] & (rank[..., None] == jnp.arange(LONG))
    index = jnp.where(term, jnp.arange(size, dtype=jnp.int32)[:, None], 0).sum(2)
    index = index.astype(jnp.int32)
    flat = jnp.transpose(rules, (0, 3, 2, 1, 4)).reshape(-1, 4, NW, size)
    chosen = jnp.where(hot[None, ..., None], flat[:, :, None], 0.0).sum(3)
    factor = jnp.where(term[None], chosen[..., None], 0.0).sum(3)
    return out.reshape(-1), index.reshape(-1), factor.reshape(rules.shape[0], -1)


def split(x):
    high = x.astype(BF16)
    return high, (x - high.astype(F32)).astype(BF16)


def mix(blocks, base, index_ref, factor_ref, first, terms):
    total = None
    for k in range(terms):
        term = blocks[base + index_ref[first + k]] * factor_ref[first + k]
        total = term if total is None else total + term
    return total


def stacked(x):
    high, low = split(x)
    row = jnp.concatenate([high, low], axis=1)
    return jnp.concatenate([row, row], axis=0)


def folded(x):
    return x[:, :TILE] + x[:, TILE:]


def dot(a, b):
    return jnp.dot(a, b, preferred_element_type=F32)


def site_kernel(
    class_ref, out_ref, index_ref, factor_ref, env_ref, k0, k1, k2, k3, k4, bra_ref, closed_ref,
    kets, product, bras,
):
    for c, ref in enumerate((k0, k1, k2, k3, k4)):
        for t in range(4):
            high, low = split(ref[t])
            kets[c, t * TILE : (t + 1) * TILE, :TILE] = high
            kets[c, t * TILE : (t + 1) * TILE, TILE:] = low
    for s in range(4):
        bras[s] = stacked(bra_ref[s])

    def form(w, carry):
        result = folded(dot(kets[class_ref[w]], stacked(env_ref[w])))
        product[pl.ds(4 * w, 4)] = result.reshape(4, TILE, TILE)
        return carry

    lax.fori_loop(0, NW, form, 0)

    def close(s, terms, i, carry):
        place = s * NW + i
        high, low = split(mix(product, 0, index_ref, factor_ref, place * LONG, terms))
        result = folded(dot(jnp.concatenate([high, low], axis=1), bras[s]))
        closed_ref[s, out_ref[place]] = result
        return carry

    for s in (3, 2, 1, 0):
        lax.fori_loop(0, LONG, functools.partial(close, s, LONG), 0)
        lax.fori_loop(LONG, NW, functools.partial(close, s, SHORT), 0)


def site(env, kets, bra, channel_class, out, index, factor):
    vmem = pl.BlockSpec(memory_space=pltpu.VMEM)
    smem = pl.BlockSpec(memory_space=pltpu.SMEM)
    return pl.pallas_call(
        site_kernel,
        out_shape=jax.ShapeDtypeStruct((4, NW, TILE, TILE), F32),
        in_specs=[smem] * 4 + [vmem] * 7,
        out_specs=vmem,
        scratch_shapes=[
            pltpu.VMEM((5, 4 * TILE, 2 * TILE), BF16),
            pltpu.VMEM((4 * NW, TILE, TILE), F32),
            pltpu.VMEM((4, 2 * TILE, 2 * TILE), BF16),
        ],
        compiler_params=pltpu.CompilerParams(vmem_limit_bytes=40 * 2**20),
        cost_estimate=pl.CostEstimate(flops=4 * 10**9, bytes_accessed=7 * 10**6, transcendentals=0),
    )(channel_class, out, index, factor, env, *kets, bra)


def pair_kernel(
    class_ref, out_ref, index_ref, left_ref, right_ref, env_ref, kets_hbm, r0, r1, r2, r3, r4,
    rows_ref, cols_ref, image_ref,
    kets, rights, product, middle, outer, sems,
):
    def kets_copy(t):
        return pltpu.make_async_copy(kets_hbm.at[t], kets.at[t], sems.at[t])

    sources = ((r0, (0,)), (r1, (1,)), (r2, (2,)), (r3, (3, 6)), (r4, (4, 7, 5, 8)))
    rights_copies = [
        pltpu.make_async_copy(ref.at[n], rights.at[step], sems.at[4 + step])
        for ref, held in sources
        for n, step in enumerate(held)
    ]
    for t in range(4):
        kets_copy(t).start()
    for copy in rights_copies:
        copy.start()

    for t2 in range(4):
        kets_copy(t2).wait()

        def form(w, carry):
            result = folded(dot(kets[t2, class_ref[w]], stacked(env_ref[w])))
            product[pl.ds(4 * w, 4)] = result.reshape(4, TILE, TILE)
            return carry

        lax.fori_loop(0, NW, form, 0)

        def left(s, terms, i, carry):
            place = s * NW + i
            total = mix(product, 0, index_ref, left_ref, place * LONG, terms)
            middle[s * 4 * NW + 4 * out_ref[place] + t2] = total
            return carry

        for s in range(4):
            lax.fori_loop(0, LONG, functools.partial(left, s, LONG), 0)
            lax.fori_loop(LONG, NW, functools.partial(left, s, SHORT), 0)

    for copy in rights_copies:
        copy.wait()
    for s1 in range(4):
        for s2 in range(4):
            def right(terms, i, carry):
                place = s2 * NW + i
                total = mix(middle, s1 * 4 * NW, index_ref, right_ref, place * LONG, terms)
                high, low = split(total)
                row = pl.ds(pl.multiple_of(out_ref[place] * TILE, TILE), TILE)
                outer[row, :TILE] = high
                outer[row, TILE:] = low
                return carry

            lax.fori_loop(0, LONG, functools.partial(right, LONG), 0)
            lax.fori_loop(LONG, NW, functools.partial(right, SHORT), 0)
            step = NEEDED.index(STATE_STEPS[s1] + STATE_STEPS[s2])
            total = dot(rights[step], outer[...])
            total = folded(total[:TILE] + total[TILE:])
            p = 4 * s1 + s2
            image_ref[p] = total.T * rows_ref[...] * cols_ref[p : p + 1]


def pair(env, kets, rights, rows, cols, channel_class, out, index, left, right):
    vmem = pl.BlockSpec(memory_space=pltpu.VMEM)
    smem = pl.BlockSpec(memory_space=pltpu.SMEM)
    hbm = pl.BlockSpec(memory_space=pl.ANY)
    return pl.pallas_call(
        pair_kernel,
        out_shape=jax.ShapeDtypeStruct((16, TILE, TILE), F32),
        in_specs=[smem] * 5 + [vmem, hbm] + [hbm] * 5 + [vmem, vmem],
        out_specs=vmem,
        scratch_shapes=[
            pltpu.VMEM((4, 5, 4 * TILE, 2 * TILE), BF16),
            pltpu.VMEM((9, 2 * TILE, NW * TILE), BF16),
            pltpu.VMEM((4 * NW, TILE, TILE), F32),
            pltpu.VMEM((16 * NW, TILE, TILE), F32),
            pltpu.VMEM((NW * TILE, 2 * TILE), BF16),
            pltpu.SemaphoreType.DMA((13,)),
        ],
        compiler_params=pltpu.CompilerParams(vmem_limit_bytes=58 * 2**20),
        cost_estimate=pl.CostEstimate(flops=20 * 10**9, bytes_accessed=18 * 10**6, transcendentals=0),
        name="pair",
    )(channel_class, out, index, left, right, env, kets, *rights, rows, cols)


def rights_kernel(x_ref, out_ref):
    for x in range(NW):
        high, low = split(x_ref[0, x])
        out_ref[0, :TILE, x * TILE : (x + 1) * TILE] = high
        out_ref[0, TILE:, x * TILE : (x + 1) * TILE] = low


def split_rights(x):
    n = x.shape[0]
    return pl.pallas_call(
        rights_kernel,
        grid=(n,),
        out_shape=jax.ShapeDtypeStruct((n, 2 * TILE, NW * TILE), BF16),
        in_specs=[pl.BlockSpec((1, NW, TILE, TILE), lambda i: (i, 0, 0, 0))],
        out_specs=pl.BlockSpec((1, 2 * TILE, NW * TILE), lambda i: (i, 0, 0)),
        cost_estimate=pl.CostEstimate(flops=n * 10**6, bytes_accessed=n * 2228224, transcendentals=0),
        name="split_rights",
    )(x)


def kets_kernel(k0, k1, k2, k3, k4, out_ref):
    for c, ref in enumerate((k0, k1, k2, k3, k4)):
        for t1 in range(4):
            high, low = split(ref[t1, 0])
            out_ref[0, c, t1 * TILE : (t1 + 1) * TILE, :TILE] = high
            out_ref[0, c, t1 * TILE : (t1 + 1) * TILE, TILE:] = low


def split_kets(kets):
    return pl.pallas_call(
        kets_kernel,
        grid=(4,),
        out_shape=jax.ShapeDtypeStruct((4, 5, 4 * TILE, 2 * TILE), BF16),
        in_specs=[pl.BlockSpec((4, 1, TILE, TILE), lambda i: (0, i, 0, 0))] * 5,
        out_specs=pl.BlockSpec((1, 5, 4 * TILE, 2 * TILE), lambda i: (i, 0, 0, 0)),
        cost_estimate=pl.CostEstimate(flops=5 * 10**6, bytes_accessed=10**7, transcendentals=0),
        name="split_kets",
    )(*[k.reshape(4, 4, TILE, TILE) for k in kets])


def fetch(blocks, offset, axis="block"):
    length = lax.axis_size(axis)
    pairs = [(i, i - offset) for i in range(length) if 0 <= i - offset < length]
    return lax.ppermute(blocks, axis, pairs)


def inside(sector, offsets):
    target = sector + offsets
    return ((target >= 0) & (target < NSEC)).astype(F32)


def live(count, sectors):
    held = jnp.where(inside(sectors, 0) > 0, jnp.take(count, jnp.clip(sectors, 0, NSEC - 1)), 0)
    return (jnp.arange(TILE, dtype=jnp.int32)[None, :] < held[:, None]).astype(F32)


def shards(
    env_left,
    env_right,
    site_tensors,
    pair_state,
    mpo_sites,
    mpo_pair,
    channel_class,
    live_rows,
    region_sites,
):
    sector = lax.axis_index("block")
    shifts = jnp.take(jnp.array(CLASS_STEPS, dtype=jnp.int32), channel_class)
    pair_steps = jnp.array(PAIR_STEPS, dtype=jnp.int32)
    env_keep = inside(sector, shifts)[:, None, None]
    state_keep = inside(sector, jnp.array(STATE_STEPS, dtype=jnp.int32))[None, :, None, None]
    tensors = site_tensors[0, :, :, 0] * state_keep
    turned = jnp.swapaxes(tensors, -1, -2)

    near = [turned] + [fetch(turned, step) for step in (ND, -ND, 1, -1)]
    near = [near[0], near[3], near[4], near[1], near[2]]

    start = jnp.swapaxes(env_left[0, :, 0] * env_keep, -1, -2)
    pair_blocks = jnp.swapaxes(pair_state[0, :, 0] * inside(sector, pair_steps)[:, None, None], -1, -2)
    right = env_right[0, :, 0] * env_keep
    side = fetch(jnp.concatenate([pair_blocks, right]), 1)
    kets2 = fetch(pair_blocks, -1)
    kets4 = fetch(pair_blocks, -ND)
    right_8 = fetch(right, ND)
    right_2 = fetch(side[16:], 1)
    right_16 = fetch(right_8, ND)
    kets3 = fetch(pair_blocks, ND)
    far = jnp.stack([right_8, right_16])
    far_1 = fetch(far, 1)
    far_2 = fetch(far_1, 1)

    rules = jnp.concatenate([mpo_sites[0], mpo_pair[0]])
    out, index, factor = mix_tables(channel_class, rules)

    def closed_blocks(i, environment):
        return site(
            environment, [k[i] for k in near], tensors[i], channel_class, out, index, factor[i]
        )

    def masks(i):
        rows = live(live_rows[0, i], sector[None])
        columns = live(live_rows[0, i], sector + shifts)
        return columns[:, :, None] * rows[0]

    closed = closed_blocks(0, start)
    below3 = fetch(closed[3], -1)
    below2 = fetch(closed[2], -1)
    partial = fetch(closed[1] + below3, -ND)
    first = (closed[0] + below2 + partial) * masks(0)

    closed = closed_blocks(1, first)
    below3 = fetch(closed[3], -1)
    below2 = fetch(closed[2], -1)
    upper = closed[1] + below3
    lower = closed[0] + below2
    keep = masks(1)
    parts = []
    passed = []
    for lo, hi in ((0, 9), (9, NW)):
        partial = fetch(upper[lo:hi], -ND)
        second = (lower[lo:hi] + partial) * keep[lo:hi]
        second = jnp.where(region_sites[0] > 1, second, first[lo:hi])
        parts.append(second)
        passed.append(fetch(second, -1, "region"))
    environment = jnp.swapaxes(jnp.concatenate(parts), -1, -2)
    boundary = jnp.where(lax.axis_index("region") == 0, start, jnp.concatenate(passed))

    rights = [split_rights(x) for x in (right[None], side[None, 16:], right_2[None], far)]
    rights.append(split_rights(jnp.concatenate([far_1, far_2])))
    kets = split_kets([pair_blocks, side[:16], kets2, kets3, kets4])
    images = pair(
        boundary,
        kets,
        rights,
        live(live_rows[0, MAXLEN], sector[None]).reshape(TILE, 1),
        live(live_rows[0, MAXLEN], sector + pair_steps),
        channel_class,
        out,
        index,
        factor[2],
        factor[3],
    )
    return environment[None, :, None], images[None, :, None]


def solution(mesh):
    in_specs = (
        P("region", None, "block", None, None),
        P("region", None, "block", None, None),
        P("region", None, None, "block", None, None),
        P("region", None, "block", None, None),
        P("region", None, None, None, None, None),
        P("region", None, None, None, None, None),
        P(),
        P("region", None, None),
        P("region"),
    )
    out_specs = (P("region", None, "block", None, None), P("region", None, "block", None, None))
    return jax.shard_map(shards, mesh=mesh, in_specs=in_specs, out_specs=out_specs, check_vma=False)
```

```python
import functools
import jax
import jax.numpy as jnp
from jax import lax
from jax.experimental import pallas as pl
from jax.experimental.pallas import tpu as pltpu
from jax.sharding import PartitionSpec as P

NSEC = 32
TILE = 128
NW = 17
ND = 8
MAXLEN = 2
STATE_STEPS = (0, ND, 1, ND + 1)
CLASS_STEPS = (0, 1, -1, ND, -ND)
LONG = 11
SHORT = 5
RULE = NW * NW * 16
PADDED = RULE + NW * 16
F32 = jnp.float32
BF16 = jnp.bfloat16


def mix_tables(channel_class):
    steps = jnp.array(STATE_STEPS, dtype=jnp.int32)
    shifts = class_shift(channel_class)
    down = (jnp.arange(4) // 2)[:, None]
    up = (jnp.arange(4) % 2)[:, None]
    kind = channel_class[None, :]
    three = (
        (kind == 0)
        | ((kind == 1) & (down == 0))
        | ((kind == 2) & (down == 1))
        | ((kind == 3) & (up == 0))
        | ((kind == 4) & (up == 1))
    )
    channels = jnp.arange(NW, dtype=jnp.int32)
    key = jnp.where(three, 0, NW) + channels[None, :]
    place = (key[:, None, :] < key[:, :, None]).astype(jnp.int32).sum(-1)
    hot = place[:, None, :] == channels[None, :, None]
    out = jnp.where(hot, channels, 0).sum(-1)
    goal = jnp.where(hot, shifts, 0).sum(-1)
    source = shifts[:, None] + steps[None, :]
    allowed = (goal + steps[:, None])[:, :, None] == source.reshape(-1)[None, None, :]
    size = 4 * NW
    order = jnp.arange(size, dtype=jnp.int32)
    earlier = (order[:, None] < order[None, :]).astype(F32)
    rank = jnp.einsum("sim,mn->sin", allowed.astype(F32), earlier).astype(jnp.int32)
    term = allowed[:, :, None, :] & (rank[:, :, None, :] == jnp.arange(LONG)[:, None])
    count = allowed.astype(jnp.int32).sum(-1)
    block = jnp.where(term, order, 0).sum(-1)
    used = jnp.arange(LONG) < count[:, :, None]
    place = (block // 4) * (NW * 16) + block % 4
    place = jnp.where(used, place, RULE) + (out * 16 + 4 * jnp.arange(4)[:, None])[:, :, None]
    return out.reshape(-1), block.reshape(-1), place.reshape(-1)


def class_shift(kind):
    return jnp.where(kind == 1, 1, jnp.where(kind == 2, -1, jnp.where(kind == 3, ND, jnp.where(kind == 4, -ND, 0))))


def inside(sector):
    return ((sector >= 0) & (sector < NSEC)).astype(F32)


def split(x):
    high = x.astype(BF16)
    return high, (x - high.astype(F32)).astype(BF16)


def mix(blocks, base, block_ref, place_ref, rule_ref, rule, first, terms):
    total = None
    for k in range(terms):
        term = blocks[base + block_ref[first + k]] * rule_ref[rule * PADDED + place_ref[first + k]]
        total = term if total is None else total + term
    return total


def stacked(x):
    row = jnp.concatenate(split(x), axis=1)
    return jnp.concatenate([row, row], axis=0)


def folded(x):
    return x[:, :TILE] + x[:, TILE:]


def dot(a, b):
    return jnp.dot(a, b, preferred_element_type=F32)


def loop(start, stop, body, unroll):
    lax.fori_loop(start, stop, lambda i, c: (body(i), c)[1], 0, unroll=unroll)


def site_kernel(
    number, sector_ref, class_ref, live_ref, out_ref, block_ref, place_ref, rule_ref, *refs
):
    if number == 0:
        env_ref, *refs = refs
    else:
        low_ref, below_ref, above_ref, *refs = refs
    kets_refs, refs = refs[:5], refs[5:]
    closed_refs, refs = refs[:4], refs[4:]
    if number > 0:
        first_ref, *refs = refs
    kets, product, bras, _ = refs
    sector = sector_ref[0]

    for c, ref in enumerate(kets_refs):
        for t in range(4):
            keep = inside(sector + CLASS_STEPS[c] + STATE_STEPS[t])
            high, low = split(ref[0, t].T * keep)
            kets[c, t * TILE : (t + 1) * TILE, :TILE] = high
            kets[c, t * TILE : (t + 1) * TILE, TILE:] = low
    for s in range(4):
        bras[s] = stacked(kets_refs[0][0, s] * inside(sector + STATE_STEPS[s]))

    rows = lax.broadcasted_iota(jnp.int32, (TILE, TILE), 1)
    columns = lax.broadcasted_iota(jnp.int32, (TILE, TILE), 0)

    def environment(w):
        ket = sector + class_shift(class_ref[w])
        keep = inside(ket)
        if number == 0:
            return (env_ref[w] * keep).T
        count = jnp.where(keep > 0, live_ref[(number - 1) * NSEC + jnp.clip(ket, 0, NSEC - 1)], 0)
        own = live_ref[(number - 1) * NSEC + sector]
        total = low_ref[w] + below_ref[w] + above_ref[w]
        total = jnp.where((rows < own) & (columns < count), total, 0.0)
        first_ref[w] = total
        return total

    def form(w):
        result = folded(dot(kets[class_ref[w]], stacked(environment(w))))
        product[pl.ds(4 * w, 4)] = result.reshape(4, TILE, TILE)

    loop(0, NW, form, 1)

    for s in (3, 2, 1, 0):

        def close(terms, i):
            place = s * NW + i
            total = mix(product, 0, block_ref, place_ref, rule_ref, number, place * LONG, terms)
            result = folded(dot(jnp.concatenate(split(total), axis=1), bras[s]))
            closed_refs[s][out_ref[place]] = result

        loop(0, LONG, functools.partial(close, LONG), UNROLL_LONG)
        loop(LONG, NW, functools.partial(close, SHORT), UNROLL_SHORT)


UNROLL_LONG = 11
UNROLL_SHORT = 6
SMEM_SPEC = pl.BlockSpec(memory_space=pltpu.SMEM)
VMEM_SPEC = pl.BlockSpec(memory_space=pltpu.VMEM)
HBM_SPEC = pl.BlockSpec(memory_space=pl.ANY)


def site(number, scalars, envs, kets):
    block = jax.ShapeDtypeStruct((NW, TILE, TILE), F32)
    count = 4 if number == 0 else 5
    ket_spec = pl.BlockSpec((1, 4, TILE, TILE), lambda i: (number, 0, 0, 0))
    return pl.pallas_call(
        functools.partial(site_kernel, number),
        grid=(1,),
        out_shape=[block] * count,
        in_specs=[SMEM_SPEC] * 7 + [VMEM_SPEC] * len(envs) + [ket_spec] * 5,
        out_specs=[VMEM_SPEC] * count,
        scratch_shapes=[
            pltpu.VMEM((5, 4 * TILE, 2 * TILE), BF16),
            pltpu.VMEM((4 * NW, TILE, TILE), F32),
            pltpu.VMEM((4, 2 * TILE, 2 * TILE), BF16),
            pltpu.VMEM((2 * TILE, 2 * TILE), BF16),
        ],
        compiler_params=pltpu.CompilerParams(vmem_limit_bytes=40 * 2**20),
        cost_estimate=pl.CostEstimate(flops=4 * 10**9, bytes_accessed=10**7, transcendentals=0),
    )(*scalars, *envs, *kets)


def kets_kernel(sector_ref, k0, k1, k2, k3, k4, out_ref):
    t2 = pl.program_id(0)
    step2 = (t2 % 2) * ND + t2 // 2
    for c, ref in enumerate((k0, k1, k2, k3, k4)):
        for t1 in range(4):
            keep = inside(sector_ref[0] + CLASS_STEPS[c] + STATE_STEPS[t1] + step2)
            high, low = split(ref[t1, 0].T * keep)
            out_ref[0, c, t1 * TILE : (t1 + 1) * TILE, :TILE] = high
            out_ref[0, c, t1 * TILE : (t1 + 1) * TILE, TILE:] = low


def split_kets(sector, kets):
    return pl.pallas_call(
        kets_kernel,
        grid=(4,),
        out_shape=jax.ShapeDtypeStruct((4, 5, 4 * TILE, 2 * TILE), BF16),
        in_specs=[SMEM_SPEC] + [pl.BlockSpec((4, 1, TILE, TILE), lambda i: (0, i, 0, 0))] * 5,
        out_specs=pl.BlockSpec((1, 5, 4 * TILE, 2 * TILE), lambda i: (i, 0, 0, 0)),
        cost_estimate=pl.CostEstimate(flops=5 * 10**6, bytes_accessed=10**7, transcendentals=0),
        name="split_kets",
    )(sector, *[k.reshape(4, 4, TILE, TILE) for k in kets])


def pair_kernel(
    sector_ref, region_ref, class_ref, live_ref, out_ref, block_ref, place_ref, rule_ref, p_ref,
    start_ref, passed0_ref, passed1_ref, kets_hbm, *refs,
):
    rights_hbm, (image_ref, kets, rights, envs, product, middle, lhs, outer, sems) = refs[:9], refs[9:]
    sector = sector_ref[0]

    def kets_copy(t):
        return pltpu.make_async_copy(kets_hbm.at[t], kets.at[t], sems.at[t])

    rights_copies = [
        pltpu.make_async_copy(ref, rights.at[n], sems.at[4 + n]) for n, ref in enumerate(rights_hbm)
    ]
    for t in range(4):
        kets_copy(t).start()
    for copy in rights_copies:
        copy.start()

    @pl.when(region_ref[0] == 0)
    def _():
        def own(w):
            keep = inside(sector + class_shift(class_ref[w]))
            envs[w] = stacked((start_ref[w] * keep).T)

        loop(0, NW, own, 1)

    @pl.when(region_ref[0] != 0)
    def _():
        for first, ref in ((0, passed0_ref), (9, passed1_ref)):
            for n in range(ref.shape[0]):
                envs[first + n] = stacked(ref[n])

    def left_half(t2):
        kets_copy(t2).wait()

        def form(w):
            result = folded(dot(kets[t2, class_ref[w]], envs[w]))
            product[pl.ds(4 * w, 4)] = result.reshape(4, TILE, TILE)

        loop(0, NW, form, 1)

        def left(s):
            for i in range(NW):
                place = s * NW + i
                terms = LONG if i < LONG else SHORT
                total = mix(product, 0, block_ref, place_ref, rule_ref, 0, place * LONG, terms)
                middle[s * 4 * NW + 4 * out_ref[place] + t2] = total

        loop(0, 4, left, 1)

    loop(0, 4, left_half, 1)
    for copy in rights_copies:
        copy.wait()

    rows = lax.broadcasted_iota(jnp.int32, (TILE, TILE), 0)
    columns = lax.broadcasted_iota(jnp.int32, (TILE, TILE), 1)
    own = live_ref[MAXLEN * NSEC + sector]

    def right_half(n):
        p = p_ref[n]
        s1 = p // 4
        s2 = p % 4
        ups = s1 % 2 + s2 % 2
        downs = s1 // 2 + s2 // 2
        far = sector + ND * ups + downs
        for i in range(NW):
            place = s2 * NW + i
            x = out_ref[place]
            keep = inside(far + class_shift(class_ref[x]))
            high, low = split(rights[3 * ups + downs, x] * keep)
            lhs[:TILE, i * TILE : (i + 1) * TILE] = high
            lhs[TILE:, i * TILE : (i + 1) * TILE] = low
            terms = LONG if i < LONG else SHORT
            total = mix(middle, s1 * 4 * NW, block_ref, place_ref, rule_ref, 1, place * LONG, terms)
            high, low = split(total)
            outer[i * TILE : (i + 1) * TILE, :TILE] = high
            outer[i * TILE : (i + 1) * TILE, TILE:] = low
        total = dot(lhs[...], outer[...])
        total = folded(total[:TILE] + total[TILE:]).T
        count = jnp.where(far < NSEC, live_ref[MAXLEN * NSEC + jnp.minimum(far, NSEC - 1)], 0)
        image_ref[p] = jnp.where((rows < own) & (columns < count), total, 0.0)

    loop(0, 16, right_half, 1)


def pair(scalars, start, passed, kets, rights):
    order = jnp.arange(16, dtype=jnp.int32)
    return pl.pallas_call(
        pair_kernel,
        out_shape=jax.ShapeDtypeStruct((16, TILE, TILE), F32),
        in_specs=[SMEM_SPEC] * 9 + [VMEM_SPEC] * 3 + [HBM_SPEC] * 10,
        out_specs=VMEM_SPEC,
        scratch_shapes=[
            pltpu.VMEM((4, 5, 4 * TILE, 2 * TILE), BF16),
            pltpu.VMEM((9, NW, TILE, TILE), F32),
            pltpu.VMEM((NW, 2 * TILE, 2 * TILE), BF16),
            pltpu.VMEM((4 * NW, TILE, TILE), F32),
            pltpu.VMEM((16 * NW, TILE, TILE), F32),
            pltpu.VMEM((2 * TILE, NW * TILE), BF16),
            pltpu.VMEM((NW * TILE, 2 * TILE), BF16),
            pltpu.SemaphoreType.DMA((13,)),
        ],
        compiler_params=pltpu.CompilerParams(vmem_limit_bytes=60 * 2**20),
        cost_estimate=pl.CostEstimate(flops=20 * 10**9, bytes_accessed=18 * 10**6, transcendentals=0),
        name="pair",
    )(*scalars, order, start, *passed, kets, *rights)


def turn_kernel(e0, e1, out_ref):
    for first, ref in ((0, e0), (9, e1)):
        for n in range(ref.shape[0]):
            out_ref[first + n] = ref[n].T


def turned(parts):
    return pl.pallas_call(
        turn_kernel,
        out_shape=jax.ShapeDtypeStruct((NW, TILE, TILE), F32),
        in_specs=[VMEM_SPEC] * 2,
        out_specs=VMEM_SPEC,
        cost_estimate=pl.CostEstimate(flops=10**6, bytes_accessed=2228224, transcendentals=0),
        name="turn",
    )(*parts)


def fetch(blocks, offset, axis="block"):
    length = lax.axis_size(axis)
    pairs = [(i, i - offset) for i in range(length) if 0 <= i - offset < length]
    return lax.ppermute(blocks, axis, pairs)


def flat_rules(rules):
    return jnp.pad(rules.reshape(2, RULE), ((0, 0), (0, PADDED - RULE))).reshape(-1)


def shards(
    env_left,
    env_right,
    site_tensors,
    pair_state,
    mpo_sites,
    mpo_pair,
    channel_class,
    live_rows,
    region_sites,
):
    start = env_left[0, :, 0]
    right = env_right[0, :, 0]
    tensors = site_tensors[0, :, :, 0]
    pairs = pair_state[0, :, 0]
    sector = lax.axis_index("block").astype(jnp.int32).reshape(1)
    region = lax.axis_index("region").astype(jnp.int32).reshape(1)
    live = live_rows.reshape(-1)

    near3 = fetch(tensors, ND)
    near4 = fetch(tensors, -ND)
    near1 = fetch(tensors, 1)
    near2 = fetch(tensors, -1)
    near = [tensors, near1, near2, near3, near4]
    rights = {(0, 0): right}
    rights[1, 0] = fetch(right, ND)
    rights[0, 1] = fetch(right, 1)
    rights[0, 2] = fetch(rights[0, 1], 1)
    rights[2, 0] = fetch(rights[1, 0], ND)
    for up in (1, 2):
        for down in (1, 2):
            rights[up, down] = fetch(rights[up, down - 1], 1)
    kets = [pairs] + [fetch(pairs, CLASS_STEPS[n]) for n in range(1, 5)]

    tables = mix_tables(channel_class)
    scalars = (sector, channel_class, live, *tables)
    site_rules = flat_rules(mpo_sites)
    h0, h1, h2, h3 = site(0, (*scalars, site_rules), [start], near)
    below3 = fetch(h3, -1)
    below2 = fetch(h2, -1)
    partial = fetch(h1 + below3, -ND)

    h0, h1, h2, h3, first = site(1, (*scalars, site_rules), [h0, below2, partial], near)
    below3 = fetch(h3, -1)
    below2 = fetch(h2, -1)
    upper = h1 + below3
    ket = sector + class_shift(channel_class)
    sectors = jnp.arange(NSEC, dtype=jnp.int32)
    width = jnp.arange(TILE, dtype=jnp.int32)
    count = jnp.where(ket[:, None] == sectors, live_rows[0, 1], 0).sum(-1)
    own = jnp.where(sector == sectors, live_rows[0, 1], 0).sum()
    keep = (width[:, None] < count[:, None, None]) & (width < own)
    parts = []
    passed = []
    for lo, hi in ((0, 9), (9, NW)):
        partial = fetch(upper[lo:hi], -ND)
        second = jnp.where(keep[lo:hi], h0[lo:hi] + below2[lo:hi] + partial, 0.0)
        second = jnp.where(region_sites[0] > 1, second, first[lo:hi])
        parts.append(second)
        passed.append(fetch(second, -1, "region"))

    environment = turned(parts)
    split = split_kets(sector, kets)
    scalars = (sector, region, channel_class, live, *tables, flat_rules(mpo_pair))
    images = pair(scalars, start, passed, split, [rights[u, d] for u in range(3) for d in range(3)])
    return environment[None, :, None], images[None, :, None]


def solution(mesh):
    in_specs = (
        P("region", None, "block", None, None),
        P("region", None, "block", None, None),
        P("region", None, None, "block", None, None),
        P("region", None, "block", None, None),
        P("region", None, None, None, None, None),
        P("region", None, None, None, None, None),
        P(),
        P("region", None, None),
        P("region"),
    )
    out_specs = (P("region", None, "block", None, None), P("region", None, "block", None, None))
    return jax.shard_map(shards, mesh=mesh, in_specs=in_specs, out_specs=out_specs, check_vma=False)
```

```python
import functools
import jax
import jax.numpy as jnp
from jax import lax
from jax.experimental import pallas as pl
from jax.experimental.pallas import tpu as pltpu
from jax.sharding import PartitionSpec as P

NSEC = 32
TILE = 128
NW = 17
ND = 8
MAXLEN = 2
STATE_STEPS = (0, ND, 1, ND + 1)
CLASS_STEPS = (0, 1, -1, ND, -ND)
LONG = 11
SHORT = 5
RULE = NW * NW * 16
PADDED = RULE + NW * 16
F32 = jnp.float32
BF16 = jnp.bfloat16


def mix_tables(channel_class):
    steps = jnp.array(STATE_STEPS, dtype=jnp.int32)
    shifts = class_shift(channel_class)
    source = (shifts[:, None] + steps[None, :]).reshape(-1)
    goal = (jnp.array(CLASS_STEPS, dtype=jnp.int32)[:, None] + steps[None, :]).reshape(-1)
    order = jnp.arange(4 * NW, dtype=jnp.int32)
    allowed = goal[:, None] == source[None, :]
    earlier = allowed[:, None, :] & (order[None, :] < order[:, None])
    rank = earlier.astype(jnp.int32).sum(-1)
    term = allowed[:, None, :] & (rank[:, None, :] == jnp.arange(LONG, dtype=jnp.int32)[:, None])
    block = jnp.where(term, order, 0).sum(-1)
    place = jnp.where(term, (order // 4) * (NW * 16) + order % 4 - RULE, 0).sum(-1) + RULE

    down = (jnp.arange(4) // 2)[:, None]
    up = (jnp.arange(4) % 2)[:, None]
    kind = channel_class[None, :]
    three = (
        (kind == 0)
        | ((kind == 1) & (down == 0))
        | ((kind == 2) & (down == 1))
        | ((kind == 3) & (up == 0))
        | ((kind == 4) & (up == 1))
    )
    channels = jnp.arange(NW, dtype=jnp.int32)
    key = jnp.where(three, 0, NW) + channels[None, :]
    position = (key[:, None, :] < key[:, :, None]).astype(jnp.int32).sum(-1)
    out = jnp.where(position[:, None, :] == channels[:, None], channels, 0).sum(-1)
    return out.reshape(-1), block.reshape(-1), place.reshape(-1)


def class_shift(kind):
    return jnp.where(kind == 1, 1, jnp.where(kind == 2, -1, jnp.where(kind == 3, ND, jnp.where(kind == 4, -ND, 0))))


def inside(sector):
    return ((sector >= 0) & (sector < NSEC)).astype(F32)


def split(x):
    high = x.astype(BF16)
    return high, (x - high.astype(F32)).astype(BF16)


def mix(blocks, base, block_ref, place_ref, rule_ref, v, kind, s, terms):
    first = (4 * kind + s) * LONG
    shift = 16 * v + 4 * s
    total = None
    for k in range(terms):
        term = blocks[base + block_ref[first + k]] * rule_ref[place_ref[first + k] + shift]
        total = term if total is None else total + term
    return total


def stacked(x):
    row = jnp.concatenate(split(x), axis=1)
    return jnp.concatenate([row, row], axis=0)


def folded(x):
    return x[:, :TILE] + x[:, TILE:]


def dot(a, b):
    return jnp.dot(a, b, preferred_element_type=F32)


def loop(start, stop, body, unroll):
    lax.fori_loop(start, stop, lambda i, c: (body(i), c)[1], 0, unroll=unroll)


def site_kernel(
    number, sector_ref, class_ref, live_ref, out_ref, block_ref, place_ref, rule_ref, *refs
):
    if number == 0:
        env_ref, *refs = refs
    else:
        low_ref, below_ref, above_ref, *refs = refs
    kets_refs, refs = refs[:5], refs[5:]
    closed_refs, refs = refs[:4], refs[4:]
    if number > 0:
        first_ref, *refs = refs
    kets, product, bras, _ = refs
    sector = sector_ref[0]

    for c, ref in enumerate(kets_refs):
        for t in range(4):
            keep = inside(sector + CLASS_STEPS[c] + STATE_STEPS[t])
            high, low = split(ref[0, t].T * keep)
            kets[c, t * TILE : (t + 1) * TILE, :TILE] = high
            kets[c, t * TILE : (t + 1) * TILE, TILE:] = low
    for s in range(4):
        bras[s] = stacked(kets_refs[0][0, s] * inside(sector + STATE_STEPS[s]))

    rows = lax.broadcasted_iota(jnp.int32, (TILE, TILE), 1)
    columns = lax.broadcasted_iota(jnp.int32, (TILE, TILE), 0)

    def environment(w):
        ket = sector + class_shift(class_ref[w])
        keep = inside(ket)
        if number == 0:
            return (env_ref[w] * keep).T
        count = jnp.where(keep > 0, live_ref[(number - 1) * NSEC + jnp.clip(ket, 0, NSEC - 1)], 0)
        own = live_ref[(number - 1) * NSEC + sector]
        total = low_ref[w] + below_ref[w] + above_ref[w]
        total = jnp.where((rows < own) & (columns < count), total, 0.0)
        first_ref[w] = total
        return total

    def form(w):
        result = folded(dot(kets[class_ref[w]], stacked(environment(w))))
        product[pl.ds(4 * w, 4)] = result.reshape(4, TILE, TILE)

    loop(0, NW, form, 1)

    for s in (3, 2, 1, 0):

        def close(terms, i):
            v = out_ref[s * NW + i]
            total = mix(product, 0, block_ref, place_ref, rule_ref, v, class_ref[v], s, terms)
            result = folded(dot(jnp.concatenate(split(total), axis=1), bras[s]))
            closed_refs[s][v] = result

        loop(0, LONG, functools.partial(close, LONG), UNROLL_LONG)
        loop(LONG, NW, functools.partial(close, SHORT), UNROLL_SHORT)


UNROLL_LONG = 11
UNROLL_SHORT = 6
SMEM_SPEC = pl.BlockSpec(memory_space=pltpu.SMEM)
VMEM_SPEC = pl.BlockSpec(memory_space=pltpu.VMEM)
HBM_SPEC = pl.BlockSpec(memory_space=pl.ANY)


def site(number, scalars, envs, kets):
    block = jax.ShapeDtypeStruct((NW, TILE, TILE), F32)
    count = 4 if number == 0 else 5
    ket_spec = pl.BlockSpec((1, 4, TILE, TILE), lambda i: (number, 0, 0, 0))
    return pl.pallas_call(
        functools.partial(site_kernel, number),
        grid=(1,),
        out_shape=[block] * count,
        in_specs=[SMEM_SPEC] * 7 + [VMEM_SPEC] * len(envs) + [ket_spec] * 5,
        out_specs=[VMEM_SPEC] * count,
        scratch_shapes=[
            pltpu.VMEM((5, 4 * TILE, 2 * TILE), BF16),
            pltpu.VMEM((4 * NW, TILE, TILE), F32),
            pltpu.VMEM((4, 2 * TILE, 2 * TILE), BF16),
            pltpu.VMEM((2 * TILE, 2 * TILE), BF16),
        ],
        compiler_params=pltpu.CompilerParams(vmem_limit_bytes=40 * 2**20),
        cost_estimate=pl.CostEstimate(flops=4 * 10**9, bytes_accessed=10**7, transcendentals=0),
    )(*scalars, *envs, *kets)


def kets_kernel(sector_ref, k0, k1, k2, k3, k4, out_ref):
    t2 = pl.program_id(0)
    step2 = (t2 % 2) * ND + t2 // 2
    for c, ref in enumerate((k0, k1, k2, k3, k4)):
        for t1 in range(4):
            keep = inside(sector_ref[0] + CLASS_STEPS[c] + STATE_STEPS[t1] + step2)
            high, low = split(ref[t1, 0].T * keep)
            out_ref[0, c, t1 * TILE : (t1 + 1) * TILE, :TILE] = high
            out_ref[0, c, t1 * TILE : (t1 + 1) * TILE, TILE:] = low


def split_kets(sector, kets):
    return pl.pallas_call(
        kets_kernel,
        grid=(4,),
        out_shape=jax.ShapeDtypeStruct((4, 5, 4 * TILE, 2 * TILE), BF16),
        in_specs=[SMEM_SPEC] + [pl.BlockSpec((4, 1, TILE, TILE), lambda i: (0, i, 0, 0))] * 5,
        out_specs=pl.BlockSpec((1, 5, 4 * TILE, 2 * TILE), lambda i: (i, 0, 0, 0)),
        cost_estimate=pl.CostEstimate(flops=5 * 10**6, bytes_accessed=10**7, transcendentals=0),
        name="split_kets",
    )(sector, *[k.reshape(4, 4, TILE, TILE) for k in kets])


def pair_kernel(
    sector_ref, region_ref, class_ref, live_ref, out_ref, block_ref, place_ref, left_ref, right_ref,
    start_ref, passed0_ref, passed1_ref, kets_hbm, *refs,
):
    rights_hbm = refs[:9]
    image_ref, kets, arrived, rights, envs, even, odd, middle, outer, sems = refs[9:]
    sector = sector_ref[0]

    def kets_copy(t):
        return pltpu.make_async_copy(kets_hbm.at[t], kets.at[t], sems.at[t])

    def rights_copy(n):
        return pltpu.make_async_copy(rights_hbm[n], arrived.at[n % 2], sems.at[4 + n % 2])

    for t in range(4):
        kets_copy(t).start()
    for n in range(2):
        rights_copy(n).start()

    @pl.when(region_ref[0] == 0)
    def _():
        def own(w):
            keep = inside(sector + class_shift(class_ref[w]))
            envs[w] = stacked((start_ref[w] * keep).T)

        loop(0, NW, own, 1)

    @pl.when(region_ref[0] != 0)
    def _():
        for first, ref in ((0, passed0_ref), (9, passed1_ref)):
            for n in range(ref.shape[0]):
                envs[first + n] = stacked(ref[n])

    def form(product, t2, w):
        result = folded(dot(kets[t2, class_ref[w]], envs[w]))
        product[pl.ds(4 * w, 4)] = result.reshape(4, TILE, TILE)

    def left(product, t2, s, i):
        v = out_ref[s * NW + i]
        terms = LONG if i < LONG else SHORT
        total = mix(product, 0, block_ref, place_ref, left_ref, v, class_ref[v], s, terms)
        middle[s * 4 * NW + 4 * v + t2] = total

    kets_copy(0).wait()
    loop(0, NW, functools.partial(form, even, 0), 1)
    for n in range(9):
        rights_copy(n).wait()

        def cut(x):
            ups, downs = n // 3, n % 3
            keep = inside(sector + ND * ups + downs + class_shift(class_ref[x]))
            rights[n, x] = jnp.concatenate(split(arrived[n % 2, x] * keep), axis=0)

        loop(0, NW, cut, 1)
        if n + 2 < 9:
            rights_copy(n + 2).start()
    for t in range(1, 4):
        kets_copy(t).wait()

    def stage(here, there, t2):
        later = jnp.minimum(t2 + 1, 3)

        def step(s):
            for i in range(NW):
                left(here, t2, s, i)
                if i % 4 == 0:
                    form(there, later, jnp.minimum(5 * s + i // 4, NW - 1))

        loop(0, 4, step, 1)

    def stages(half):
        stage(even, odd, 2 * half)
        stage(odd, even, 2 * half + 1)

    loop(0, 2, stages, 1)

    rows = lax.broadcasted_iota(jnp.int32, (TILE, TILE), 0)
    columns = lax.broadcasted_iota(jnp.int32, (TILE, TILE), 1)
    own = live_ref[MAXLEN * NSEC + sector]

    def right_half(p):
        s1 = p // 4
        s2 = p % 4
        ups = s1 % 2 + s2 % 2
        downs = s1 // 2 + s2 // 2
        far = sector + ND * ups + downs
        lhs = []
        for i in range(NW):
            x = out_ref[s2 * NW + i]
            lhs.append(rights[3 * ups + downs, x])
            terms = LONG if i < LONG else SHORT
            total = mix(middle, s1 * 4 * NW, block_ref, place_ref, right_ref, x, class_ref[x], s2, terms)
            high, low = split(total)
            outer[i * TILE : (i + 1) * TILE, :TILE] = high
            outer[i * TILE : (i + 1) * TILE, TILE:] = low
        total = dot(jnp.concatenate(lhs, axis=1), outer[...])
        total = folded(total[:TILE] + total[TILE:]).T
        count = jnp.where(far < NSEC, live_ref[MAXLEN * NSEC + jnp.minimum(far, NSEC - 1)], 0)
        image_ref[p] = jnp.where((rows < own) & (columns < count), total, 0.0)

    loop(0, 16, right_half, 1)


def pair(scalars, start, passed, kets, rights):
    return pl.pallas_call(
        pair_kernel,
        out_shape=jax.ShapeDtypeStruct((16, TILE, TILE), F32),
        in_specs=[SMEM_SPEC] * 9 + [VMEM_SPEC] * 3 + [HBM_SPEC] * 10,
        out_specs=VMEM_SPEC,
        scratch_shapes=[
            pltpu.VMEM((4, 5, 4 * TILE, 2 * TILE), BF16),
            pltpu.VMEM((2, NW, TILE, TILE), F32),
            pltpu.VMEM((9, NW, 2 * TILE, TILE), BF16),
            pltpu.VMEM((NW, 2 * TILE, 2 * TILE), BF16),
            pltpu.VMEM((4 * NW, TILE, TILE), F32),
            pltpu.VMEM((4 * NW, TILE, TILE), F32),
            pltpu.VMEM((16 * NW, TILE, TILE), F32),
            pltpu.VMEM((NW * TILE, 2 * TILE), BF16),
            pltpu.SemaphoreType.DMA((6,)),
        ],
        compiler_params=pltpu.CompilerParams(vmem_limit_bytes=60 * 2**20),
        cost_estimate=pl.CostEstimate(flops=20 * 10**9, bytes_accessed=18 * 10**6, transcendentals=0),
        name="pair",
    )(*scalars, start, *passed, kets, *rights)


def turn_kernel(e0, e1, out_ref):
    for first, ref in ((0, e0), (9, e1)):
        for n in range(ref.shape[0]):
            out_ref[first + n] = ref[n].T


def turned(parts):
    return pl.pallas_call(
        turn_kernel,
        out_shape=jax.ShapeDtypeStruct((NW, TILE, TILE), F32),
        in_specs=[VMEM_SPEC] * 2,
        out_specs=VMEM_SPEC,
        cost_estimate=pl.CostEstimate(flops=10**6, bytes_accessed=2228224, transcendentals=0),
        name="turn",
    )(*parts)


def fetch(blocks, offset, axis="block"):
    length = lax.axis_size(axis)
    pairs = [(i, i - offset) for i in range(length) if 0 <= i - offset < length]
    return lax.ppermute(blocks, axis, pairs)


def flat_rule(rule):
    return jnp.pad(rule.reshape(RULE), (0, PADDED - RULE))


def shards(
    env_left,
    env_right,
    site_tensors,
    pair_state,
    mpo_sites,
    mpo_pair,
    channel_class,
    live_rows,
    region_sites,
):
    start = env_left[0, :, 0]
    right = env_right[0, :, 0]
    tensors = site_tensors[0, :, :, 0]
    pairs = pair_state[0, :, 0]
    sector = lax.axis_index("block").astype(jnp.int32).reshape(1)
    region = lax.axis_index("region").astype(jnp.int32).reshape(1)
    live = live_rows.reshape(-1)

    near3 = fetch(tensors, ND)
    near4 = fetch(tensors, -ND)
    near1 = fetch(tensors, 1)
    near2 = fetch(tensors, -1)
    near = [tensors, near1, near2, near3, near4]
    rights = {(0, 0): right}
    rights[1, 0] = fetch(right, ND)
    rights[0, 1] = fetch(right, 1)
    rights[0, 2] = fetch(rights[0, 1], 1)
    rights[2, 0] = fetch(rights[1, 0], ND)
    for up in (1, 2):
        for down in (1, 2):
            rights[up, down] = fetch(rights[up, down - 1], 1)
    kets = [pairs] + [fetch(pairs, CLASS_STEPS[n]) for n in range(1, 5)]

    tables = mix_tables(channel_class)
    scalars = (sector, channel_class, live, *tables)
    h0, h1, h2, h3 = site(0, (*scalars, flat_rule(mpo_sites[0, 0])), [start], near)
    below3 = fetch(h3, -1)
    below2 = fetch(h2, -1)
    partial = fetch(h1 + below3, -ND)

    h0, h1, h2, h3, first = site(1, (*scalars, flat_rule(mpo_sites[0, 1])), [h0, below2, partial], near)
    below3 = fetch(h3, -1)
    below2 = fetch(h2, -1)
    upper = h1 + below3
    ket = sector + class_shift(channel_class)
    sectors = jnp.arange(NSEC, dtype=jnp.int32)
    width = jnp.arange(TILE, dtype=jnp.int32)
    count = jnp.where(ket[:, None] == sectors, live_rows[0, 1], 0).sum(-1)
    own = jnp.where(sector == sectors, live_rows[0, 1], 0).sum()
    keep = (width[:, None] < count[:, None, None]) & (width < own)
    parts = []
    passed = []
    for lo, hi in ((0, 9), (9, NW)):
        partial = fetch(upper[lo:hi], -ND)
        second = jnp.where(keep[lo:hi], h0[lo:hi] + below2[lo:hi] + partial, 0.0)
        second = jnp.where(region_sites[0] > 1, second, first[lo:hi])
        parts.append(second)
        passed.append(fetch(second, -1, "region"))

    environment = turned(parts)
    split = split_kets(sector, kets)
    scalars = (sector, region, channel_class, live, *tables, flat_rule(mpo_pair[0, 0]), flat_rule(mpo_pair[0, 1]))
    images = pair(scalars, start, passed, split, [rights[u, d] for u in range(3) for d in range(3)])
    return environment[None, :, None], images[None, :, None]


def solution(mesh):
    in_specs = (
        P("region", None, "block", None, None),
        P("region", None, "block", None, None),
        P("region", None, None, "block", None, None),
        P("region", None, "block", None, None),
        P("region", None, None, None, None, None),
        P("region", None, None, None, None, None),
        P(),
        P("region", None, None),
        P("region"),
    )
    out_specs = (P("region", None, "block", None, None), P("region", None, "block", None, None))
    return jax.shard_map(shards, mesh=mesh, in_specs=in_specs, out_specs=out_specs, check_vma=False)
```

```python
import functools
import jax
import jax.numpy as jnp
from jax import lax
from jax.experimental import pallas as pl
from jax.experimental.pallas import tpu as pltpu
from jax.sharding import PartitionSpec as P

NSEC = 32
TILE = 128
NW = 17
ND = 8
MAXLEN = 2
STATE_STEPS = (0, ND, 1, ND + 1)
CLASS_STEPS = (0, 1, -1, ND, -ND)
LONG = 11
SHORT = 5
RULE = NW * NW * 16
PADDED = RULE + NW * 16
F32 = jnp.float32
BF16 = jnp.bfloat16


def mix_tables(channel_class):
    steps = jnp.array(STATE_STEPS, dtype=jnp.int32)
    shifts = class_shift(channel_class)
    source = (shifts[:, None] + steps[None, :]).reshape(-1)
    goal = (jnp.array(CLASS_STEPS, dtype=jnp.int32)[:, None] + steps[None, :]).reshape(-1)
    order = jnp.arange(4 * NW, dtype=jnp.int32)
    allowed = goal[:, None] == source[None, :]
    earlier = allowed[:, None, :] & (order[None, :] < order[:, None])
    rank = earlier.astype(jnp.int32).sum(-1)
    term = allowed[:, None, :] & (rank[:, None, :] == jnp.arange(LONG, dtype=jnp.int32)[:, None])
    block = jnp.where(term, order, 0).sum(-1)
    place = jnp.where(term, (order // 4) * (NW * 16) + order % 4 - RULE, 0).sum(-1) + RULE

    down = (jnp.arange(4) // 2)[:, None]
    up = (jnp.arange(4) % 2)[:, None]
    kind = channel_class[None, :]
    three = (
        (kind == 0)
        | ((kind == 1) & (down == 0))
        | ((kind == 2) & (down == 1))
        | ((kind == 3) & (up == 0))
        | ((kind == 4) & (up == 1))
    )
    channels = jnp.arange(NW, dtype=jnp.int32)
    key = jnp.where(three, 0, NW) + channels[None, :]
    position = (key[:, None, :] < key[:, :, None]).astype(jnp.int32).sum(-1)
    out = jnp.where(position[:, None, :] == channels[:, None], channels, 0).sum(-1)
    return out.reshape(-1), block.reshape(-1), place.reshape(-1)


def class_shift(kind):
    return jnp.where(kind == 1, 1, jnp.where(kind == 2, -1, jnp.where(kind == 3, ND, jnp.where(kind == 4, -ND, 0))))


def inside(sector):
    return ((sector >= 0) & (sector < NSEC)).astype(F32)


def split(x):
    high = x.astype(BF16)
    return high, (x - high.astype(F32)).astype(BF16)


def mix(blocks, base, block_ref, place_ref, rule_ref, v, kind, s, terms):
    first = (4 * kind + s) * LONG
    shift = 16 * v + 4 * s
    total = None
    for k in range(terms):
        term = blocks[base + block_ref[first + k]] * rule_ref[place_ref[first + k] + shift]
        total = term if total is None else total + term
    return total


def stacked(x):
    row = jnp.concatenate(split(x), axis=1)
    return jnp.concatenate([row, row], axis=0)


def folded(x):
    return x[:, :TILE] + x[:, TILE:]


def dot(a, b):
    return jnp.dot(a, b, preferred_element_type=F32)


def loop(start, stop, body, unroll):
    lax.fori_loop(start, stop, lambda i, c: (body(i), c)[1], 0, unroll=unroll)


def site_kernel(
    number, sector_ref, class_ref, live_ref, out_ref, block_ref, place_ref, rule_ref, *refs
):
    if number == 0:
        env_ref, *refs = refs
    else:
        low_ref, below_ref, above_ref, *refs = refs
    kets_refs, refs = refs[:5], refs[5:]
    closed_refs, refs = refs[:4], refs[4:]
    if number > 0:
        first_ref, *refs = refs
    kets, product, bras, _ = refs
    sector = sector_ref[0]

    for c, ref in enumerate(kets_refs):
        for t in range(4):
            keep = inside(sector + CLASS_STEPS[c] + STATE_STEPS[t])
            high, low = split(ref[0, t].T * keep)
            kets[c, t * TILE : (t + 1) * TILE, :TILE] = high
            kets[c, t * TILE : (t + 1) * TILE, TILE:] = low
    for s in range(4):
        bras[s] = stacked(kets_refs[0][0, s] * inside(sector + STATE_STEPS[s]))

    rows = lax.broadcasted_iota(jnp.int32, (TILE, TILE), 1)
    columns = lax.broadcasted_iota(jnp.int32, (TILE, TILE), 0)

    def environment(w):
        ket = sector + class_shift(class_ref[w])
        keep = inside(ket)
        if number == 0:
            return (env_ref[w] * keep).T
        count = jnp.where(keep > 0, live_ref[(number - 1) * NSEC + jnp.clip(ket, 0, NSEC - 1)], 0)
        own = live_ref[(number - 1) * NSEC + sector]
        total = low_ref[w] + below_ref[w] + above_ref[w]
        total = jnp.where((rows < own) & (columns < count), total, 0.0)
        first_ref[w] = total
        return total

    def form(w):
        result = folded(dot(kets[class_ref[w]], stacked(environment(w))))
        product[pl.ds(4 * w, 4)] = result.reshape(4, TILE, TILE)

    loop(0, NW, form, 1)

    for s in (3, 2, 1, 0):

        def close(terms, i):
            v = out_ref[s * NW + i]
            total = mix(product, 0, block_ref, place_ref, rule_ref, v, class_ref[v], s, terms)
            result = folded(dot(jnp.concatenate(split(total), axis=1), bras[s]))
            closed_refs[s][v] = result

        loop(0, LONG, functools.partial(close, LONG), UNROLL_LONG)
        loop(LONG, NW, functools.partial(close, SHORT), UNROLL_SHORT)


UNROLL_LONG = 11
UNROLL_SHORT = 6
SMEM_SPEC = pl.BlockSpec(memory_space=pltpu.SMEM)
VMEM_SPEC = pl.BlockSpec(memory_space=pltpu.VMEM)
HBM_SPEC = pl.BlockSpec(memory_space=pl.ANY)


def site(number, scalars, envs, kets):
    block = jax.ShapeDtypeStruct((NW, TILE, TILE), F32)
    count = 4 if number == 0 else 5
    ket_spec = pl.BlockSpec((1, 4, TILE, TILE), lambda i: (number, 0, 0, 0))
    return pl.pallas_call(
        functools.partial(site_kernel, number),
        grid=(1,),
        out_shape=[block] * count,
        in_specs=[SMEM_SPEC] * 7 + [VMEM_SPEC] * len(envs) + [ket_spec] * 5,
        out_specs=[VMEM_SPEC] * count,
        scratch_shapes=[
            pltpu.VMEM((5, 4 * TILE, 2 * TILE), BF16),
            pltpu.VMEM((4 * NW, TILE, TILE), F32),
            pltpu.VMEM((4, 2 * TILE, 2 * TILE), BF16),
            pltpu.VMEM((2 * TILE, 2 * TILE), BF16),
        ],
        compiler_params=pltpu.CompilerParams(vmem_limit_bytes=60 * 2**20),
        cost_estimate=pl.CostEstimate(flops=4 * 10**9, bytes_accessed=10**7, transcendentals=0),
    )(*scalars, *envs, *kets)


def kets_kernel(sector_ref, k0, k1, k2, k3, k4, out_ref):
    t2 = pl.program_id(0)
    step2 = (t2 % 2) * ND + t2 // 2
    for c, ref in enumerate((k0, k1, k2, k3, k4)):
        for t1 in range(4):
            keep = inside(sector_ref[0] + CLASS_STEPS[c] + STATE_STEPS[t1] + step2)
            high, low = split(ref[t1, 0].T * keep)
            out_ref[0, c, t1 * TILE : (t1 + 1) * TILE, :TILE] = high
            out_ref[0, c, t1 * TILE : (t1 + 1) * TILE, TILE:] = low


def split_kets(sector, kets):
    return pl.pallas_call(
        kets_kernel,
        grid=(4,),
        out_shape=jax.ShapeDtypeStruct((4, 5, 4 * TILE, 2 * TILE), BF16),
        in_specs=[SMEM_SPEC] + [pl.BlockSpec((4, 1, TILE, TILE), lambda i: (0, i, 0, 0))] * 5,
        out_specs=pl.BlockSpec((1, 5, 4 * TILE, 2 * TILE), lambda i: (i, 0, 0, 0)),
        cost_estimate=pl.CostEstimate(flops=5 * 10**6, bytes_accessed=10**7, transcendentals=0),
        name="split_kets",
    )(sector, *[k.reshape(4, 4, TILE, TILE) for k in kets])


def pair_kernel(
    sector_ref, region_ref, class_ref, live_ref, out_ref, block_ref, place_ref, left_ref, right_ref,
    start_ref, passed0_ref, passed1_ref, kets_hbm, *refs,
):
    rights_hbm = refs[:9]
    image_ref, kets, arrived, rights, envs, even, odd, middle, outer, sems = refs[9:]
    sector = sector_ref[0]

    def kets_copy(t):
        return pltpu.make_async_copy(kets_hbm.at[t], kets.at[t], sems.at[t])

    def rights_copy(n):
        return pltpu.make_async_copy(rights_hbm[n], arrived.at[n % 2], sems.at[4 + n % 2])

    for t in range(4):
        kets_copy(t).start()
    for n in range(2):
        rights_copy(n).start()

    @pl.when(region_ref[0] == 0)
    def _():
        def own(w):
            keep = inside(sector + class_shift(class_ref[w]))
            envs[w] = stacked((start_ref[w] * keep).T)

        loop(0, NW, own, 1)

    @pl.when(region_ref[0] != 0)
    def _():
        for first, ref in ((0, passed0_ref), (9, passed1_ref)):
            for n in range(ref.shape[0]):
                envs[first + n] = stacked(ref[n])

    def form(product, t2, w):
        result = folded(dot(kets[t2, class_ref[w]], envs[w]))
        product[pl.ds(4 * w, 4)] = result.reshape(4, TILE, TILE)

    def left(product, t2, s, i):
        v = out_ref[s * NW + i]
        terms = LONG if i < LONG else SHORT
        total = mix(product, 0, block_ref, place_ref, left_ref, v, class_ref[v], s, terms)
        middle[s * 4 * NW + 4 * v + t2] = total

    kets_copy(0).wait()
    loop(0, NW, functools.partial(form, even, 0), 1)
    for n in range(9):
        rights_copy(n).wait()

        def cut(x):
            ups, downs = n // 3, n % 3
            keep = inside(sector + ND * ups + downs + class_shift(class_ref[x]))
            rights[n, x] = jnp.concatenate(split(arrived[n % 2, x] * keep), axis=0)

        loop(0, NW, cut, 1)
        if n + 2 < 9:
            rights_copy(n + 2).start()
    for t in range(1, 4):
        kets_copy(t).wait()

    def stage(here, there, t2):
        later = jnp.minimum(t2 + 1, 3)

        def step(s):
            for i in range(NW):
                left(here, t2, s, i)
                if i % 4 == 0:
                    form(there, later, jnp.minimum(5 * s + i // 4, NW - 1))

        loop(0, 4, step, 1)

    def stages(half):
        stage(even, odd, 2 * half)
        stage(odd, even, 2 * half + 1)

    loop(0, 2, stages, 1)

    rows = lax.broadcasted_iota(jnp.int32, (TILE, TILE), 0)
    columns = lax.broadcasted_iota(jnp.int32, (TILE, TILE), 1)
    own = live_ref[MAXLEN * NSEC + sector]

    def right_half(p):
        s1 = p // 4
        s2 = p % 4
        ups = s1 % 2 + s2 % 2
        downs = s1 // 2 + s2 // 2
        far = sector + ND * ups + downs
        lhs = []
        for i in range(NW):
            x = out_ref[s2 * NW + i]
            lhs.append(rights[3 * ups + downs, x])
            terms = LONG if i < LONG else SHORT
            total = mix(middle, s1 * 4 * NW, block_ref, place_ref, right_ref, x, class_ref[x], s2, terms)
            high, low = split(total)
            outer[i * TILE : (i + 1) * TILE, :TILE] = high
            outer[i * TILE : (i + 1) * TILE, TILE:] = low
        total = dot(jnp.concatenate(lhs, axis=1), outer[...])
        total = folded(total[:TILE] + total[TILE:]).T
        count = jnp.where(far < NSEC, live_ref[MAXLEN * NSEC + jnp.minimum(far, NSEC - 1)], 0)
        image_ref[p] = jnp.where((rows < own) & (columns < count), total, 0.0)

    loop(0, 16, right_half, 1)


def pair(scalars, start, passed, kets, rights):
    return pl.pallas_call(
        pair_kernel,
        out_shape=jax.ShapeDtypeStruct((16, TILE, TILE), F32),
        in_specs=[SMEM_SPEC] * 9 + [VMEM_SPEC] * 3 + [HBM_SPEC] * 10,
        out_specs=VMEM_SPEC,
        scratch_shapes=[
            pltpu.VMEM((4, 5, 4 * TILE, 2 * TILE), BF16),
            pltpu.VMEM((2, NW, TILE, TILE), F32),
            pltpu.VMEM((9, NW, 2 * TILE, TILE), BF16),
            pltpu.VMEM((NW, 2 * TILE, 2 * TILE), BF16),
            pltpu.VMEM((4 * NW, TILE, TILE), F32),
            pltpu.VMEM((4 * NW, TILE, TILE), F32),
            pltpu.VMEM((16 * NW, TILE, TILE), F32),
            pltpu.VMEM((NW * TILE, 2 * TILE), BF16),
            pltpu.SemaphoreType.DMA((6,)),
        ],
        compiler_params=pltpu.CompilerParams(vmem_limit_bytes=60 * 2**20),
        cost_estimate=pl.CostEstimate(flops=20 * 10**9, bytes_accessed=18 * 10**6, transcendentals=0),
        name="pair",
    )(*scalars, start, *passed, kets, *rights)


def turn_kernel(e0, e1, out_ref):
    for first, ref in ((0, e0), (9, e1)):
        for n in range(ref.shape[0]):
            out_ref[first + n] = ref[n].T


def turned(parts):
    return pl.pallas_call(
        turn_kernel,
        out_shape=jax.ShapeDtypeStruct((NW, TILE, TILE), F32),
        in_specs=[VMEM_SPEC] * 2,
        out_specs=VMEM_SPEC,
        cost_estimate=pl.CostEstimate(flops=10**6, bytes_accessed=2228224, transcendentals=0),
        name="turn",
    )(*parts)


def fetch(blocks, offset, axis="block"):
    length = lax.axis_size(axis)
    pairs = [(i, i - offset) for i in range(length) if 0 <= i - offset < length]
    return lax.ppermute(blocks, axis, pairs)


def fetch_next(sector, blocks, above):
    blocks, above = lax.optimization_barrier((blocks, above))
    given = jnp.where(sector[0] % ND == 0, above, blocks)
    pairs = [(i, i // ND * ND + (i - 1) % ND) for i in range(NSEC)]
    return lax.ppermute(given, "block", pairs)


def flat_rule(rule):
    return jnp.pad(rule.reshape(RULE), (0, PADDED - RULE))


def shards(
    env_left,
    env_right,
    site_tensors,
    pair_state,
    mpo_sites,
    mpo_pair,
    channel_class,
    live_rows,
    region_sites,
):
    start = env_left[0, :, 0]
    right = env_right[0, :, 0]
    tensors = site_tensors[0, :, :, 0]
    pairs = pair_state[0, :, 0]
    sector = lax.axis_index("block").astype(jnp.int32).reshape(1)
    region = lax.axis_index("region").astype(jnp.int32).reshape(1)
    live = live_rows.reshape(-1)

    near3 = fetch(tensors, ND)
    near4 = fetch(tensors, -ND)
    near1 = fetch(tensors, 1)
    near2 = fetch(tensors, -1)
    near = [tensors, near1, near2, near3, near4]
    rights = {(0, 0): right}
    rights[1, 0] = fetch(right, ND)
    rights[2, 0] = fetch(rights[1, 0], ND)
    rights[0, 1] = fetch_next(sector, right, rights[1, 0])
    rights[1, 1] = fetch_next(sector, rights[1, 0], rights[2, 0])
    rights[2, 1] = fetch(rights[2, 0], 1)
    rights[0, 2] = fetch_next(sector, rights[0, 1], rights[1, 1])
    rights[1, 2] = fetch_next(sector, rights[1, 1], rights[2, 1])
    rights[2, 2] = fetch(rights[2, 1], 1)
    pairs2 = fetch(pairs, -1)
    pairs3 = fetch(pairs, ND)
    pairs4 = fetch(pairs, -ND)
    pairs1 = fetch_next(sector, pairs, pairs3)
    kets = [pairs, pairs1, pairs2, pairs3, pairs4]

    tables = mix_tables(channel_class)
    scalars = (sector, channel_class, live, *tables)
    h0, h1, h2, h3 = site(0, (*scalars, flat_rule(mpo_sites[0, 0])), [start], near)
    below3 = fetch(h3, -1)
    below2 = fetch(h2, -1)
    partial = fetch(h1 + below3, -ND)

    h0, h1, h2, h3, first = site(1, (*scalars, flat_rule(mpo_sites[0, 1])), [h0, below2, partial], near)
    below3 = fetch(h3, -1)
    below2 = fetch(h2, -1)
    upper = h1 + below3
    ket = sector + class_shift(channel_class)
    sectors = jnp.arange(NSEC, dtype=jnp.int32)
    width = jnp.arange(TILE, dtype=jnp.int32)
    count = jnp.where(ket[:, None] == sectors, live_rows[0, 1], 0).sum(-1)
    own = jnp.where(sector == sectors, live_rows[0, 1], 0).sum()
    keep = (width[:, None] < count[:, None, None]) & (width < own)
    parts = []
    passed = []
    for lo, hi in ((0, 9), (9, NW)):
        partial = fetch(upper[lo:hi], -ND)
        second = jnp.where(keep[lo:hi], h0[lo:hi] + below2[lo:hi] + partial, 0.0)
        second = jnp.where(region_sites[0] > 1, second, first[lo:hi])
        parts.append(second)
        passed.append(fetch(second, -1, "region"))

    environment = turned(parts)
    split = split_kets(sector, kets)
    scalars = (sector, region, channel_class, live, *tables, flat_rule(mpo_pair[0, 0]), flat_rule(mpo_pair[0, 1]))
    images = pair(scalars, start, passed, split, [rights[u, d] for u in range(3) for d in range(3)])
    return environment[None, :, None], images[None, :, None]


def solution(mesh):
    in_specs = (
        P("region", None, "block", None, None),
        P("region", None, "block", None, None),
        P("region", None, None, "block", None, None),
        P("region", None, "block", None, None),
        P("region", None, None, None, None, None),
        P("region", None, None, None, None, None),
        P(),
        P("region", None, None),
        P("region"),
    )
    out_specs = (P("region", None, "block", None, None), P("region", None, "block", None, None))
    return jax.shard_map(shards, mesh=mesh, in_specs=in_specs, out_specs=out_specs, check_vma=False)
```

```python
import functools
import jax
import jax.numpy as jnp
from jax import lax
from jax.experimental import pallas as pl
from jax.experimental.pallas import tpu as pltpu
from jax.sharding import PartitionSpec as P

NSEC = 32
TILE = 128
NW = 17
ND = 8
MAXLEN = 2
STATE_STEPS = (0, ND, 1, ND + 1)
CLASS_STEPS = (0, 1, -1, ND, -ND)
LONG = 11
SHORT = 5
RULE = NW * NW * 16
PADDED = RULE + NW * 16
F32 = jnp.float32
BF16 = jnp.bfloat16


def mix_tables(channel_class):
    steps = jnp.array(STATE_STEPS, dtype=jnp.int32)
    shifts = class_shift(channel_class)
    source = (shifts[:, None] + steps[None, :]).reshape(-1)
    goal = (jnp.array(CLASS_STEPS, dtype=jnp.int32)[:, None] + steps[None, :]).reshape(-1)
    order = jnp.arange(4 * NW, dtype=jnp.int32)
    allowed = goal[:, None] == source[None, :]
    earlier = allowed[:, None, :] & (order[None, :] < order[:, None])
    rank = earlier.astype(jnp.int32).sum(-1)
    term = allowed[:, None, :] & (rank[:, None, :] == jnp.arange(LONG, dtype=jnp.int32)[:, None])
    block = jnp.where(term, order, 0).sum(-1)
    place = jnp.where(term, (order // 4) * (NW * 16) + order % 4 - RULE, 0).sum(-1) + RULE

    down = (jnp.arange(4) // 2)[:, None]
    up = (jnp.arange(4) % 2)[:, None]
    kind = channel_class[None, :]
    three = (
        (kind == 0)
        | ((kind == 1) & (down == 0))
        | ((kind == 2) & (down == 1))
        | ((kind == 3) & (up == 0))
        | ((kind == 4) & (up == 1))
    )
    channels = jnp.arange(NW, dtype=jnp.int32)
    key = jnp.where(three, 0, NW) + channels[None, :]
    position = (key[:, None, :] < key[:, :, None]).astype(jnp.int32).sum(-1)
    out = jnp.where(position[:, None, :] == channels[:, None], channels, 0).sum(-1)
    return out, block, place


def class_shift(kind):
    return jnp.where(kind == 1, 1, jnp.where(kind == 2, -1, jnp.where(kind == 3, ND, jnp.where(kind == 4, -ND, 0))))


def inside(sector):
    return ((sector >= 0) & (sector < NSEC)).astype(F32)


def split(x):
    high = x.astype(BF16)
    return high, (x - high.astype(F32)).astype(BF16)


def mix(blocks, base, block_ref, place_ref, rule_ref, v, kind, s, terms):
    row = 4 * kind + s
    shift = 16 * v + 4 * s
    total = None
    for k in range(terms):
        term = blocks[base + block_ref[row, k]] * rule_ref[place_ref[row, k] + shift]
        total = term if total is None else total + term
    return total


def stacked(x):
    row = jnp.concatenate(split(x), axis=1)
    return jnp.concatenate([row, row], axis=0)


def folded(x):
    return x[:, :TILE] + x[:, TILE:]


def dot(a, b):
    return jnp.dot(a, b, preferred_element_type=F32)


def loop(start, stop, body, unroll):
    lax.fori_loop(start, stop, lambda i, c: (body(i), c)[1], 0, unroll=unroll)


def site_kernel(
    number, sector_ref, class_ref, live_ref, out_ref, block_ref, place_ref, rule_ref, *refs
):
    if number == 0:
        env_ref, *refs = refs
    else:
        low_ref, below_ref, above_ref, *refs = refs
    kets_refs, refs = refs[:5], refs[5:]
    closed_refs, refs = refs[:4], refs[4:]
    if number > 0:
        first_ref, *refs = refs
    kets, product, bras, _ = refs
    sector = sector_ref[0]

    for c, ref in enumerate(kets_refs):
        for t in range(4):
            keep = inside(sector + CLASS_STEPS[c] + STATE_STEPS[t])
            high, low = split(ref[0, t].T * keep)
            kets[c, t * TILE : (t + 1) * TILE, :TILE] = high
            kets[c, t * TILE : (t + 1) * TILE, TILE:] = low
    for s in range(4):
        bras[s] = stacked(kets_refs[0][0, s] * inside(sector + STATE_STEPS[s]))

    rows = lax.broadcasted_iota(jnp.int32, (TILE, TILE), 1)
    columns = lax.broadcasted_iota(jnp.int32, (TILE, TILE), 0)

    def environment(w):
        ket = sector + class_shift(class_ref[w])
        keep = inside(ket)
        if number == 0:
            return (env_ref[w] * keep).T
        count = jnp.where(keep > 0, live_ref[0, number - 1, jnp.clip(ket, 0, NSEC - 1)], 0)
        own = live_ref[0, number - 1, sector]
        total = low_ref[w] + below_ref[w] + above_ref[w]
        total = jnp.where((rows < own) & (columns < count), total, 0.0)
        first_ref[w] = total
        return total

    def form(w):
        result = folded(dot(kets[class_ref[w]], stacked(environment(w))))
        product[pl.ds(4 * w, 4)] = result.reshape(4, TILE, TILE)

    loop(0, NW, form, 1)

    for s in (3, 2, 1, 0):

        def close(terms, i):
            v = out_ref[s, i]
            total = mix(product, 0, block_ref, place_ref, rule_ref, v, class_ref[v], s, terms)
            result = folded(dot(jnp.concatenate(split(total), axis=1), bras[s]))
            closed_refs[s][v] = result

        loop(0, LONG, functools.partial(close, LONG), UNROLL_LONG)
        loop(LONG, NW, functools.partial(close, SHORT), UNROLL_SHORT)


UNROLL_LONG = 11
UNROLL_SHORT = 6
SMEM_SPEC = pl.BlockSpec(memory_space=pltpu.SMEM)
VMEM_SPEC = pl.BlockSpec(memory_space=pltpu.VMEM)
HBM_SPEC = pl.BlockSpec(memory_space=pl.ANY)


def site(number, scalars, envs, kets):
    block = jax.ShapeDtypeStruct((NW, TILE, TILE), F32)
    count = 4 if number == 0 else 5
    ket_spec = pl.BlockSpec((1, 4, TILE, TILE), lambda i: (number, 0, 0, 0))
    return pl.pallas_call(
        functools.partial(site_kernel, number),
        grid=(1,),
        out_shape=[block] * count,
        in_specs=[SMEM_SPEC] * 7 + [VMEM_SPEC] * len(envs) + [ket_spec] * 5,
        out_specs=[VMEM_SPEC] * count,
        scratch_shapes=[
            pltpu.VMEM((5, 4 * TILE, 2 * TILE), BF16),
            pltpu.VMEM((4 * NW, TILE, TILE), F32),
            pltpu.VMEM((4, 2 * TILE, 2 * TILE), BF16),
            pltpu.VMEM((2 * TILE, 2 * TILE), BF16),
        ],
        compiler_params=pltpu.CompilerParams(vmem_limit_bytes=60 * 2**20),
        cost_estimate=pl.CostEstimate(flops=4 * 10**9, bytes_accessed=10**7, transcendentals=0),
    )(*scalars, *envs, *kets)


def kets_kernel(sector_ref, k0, k1, k2, k3, k4, out_ref):
    t2 = pl.program_id(0)
    step2 = (t2 % 2) * ND + t2 // 2
    for c, ref in enumerate((k0, k1, k2, k3, k4)):
        for t1 in range(4):
            keep = inside(sector_ref[0] + CLASS_STEPS[c] + STATE_STEPS[t1] + step2)
            high, low = split(ref[t1, 0].T * keep)
            out_ref[0, c, t1 * TILE : (t1 + 1) * TILE, :TILE] = high
            out_ref[0, c, t1 * TILE : (t1 + 1) * TILE, TILE:] = low


def split_kets(sector, kets):
    return pl.pallas_call(
        kets_kernel,
        grid=(4,),
        out_shape=jax.ShapeDtypeStruct((4, 5, 4 * TILE, 2 * TILE), BF16),
        in_specs=[SMEM_SPEC] + [pl.BlockSpec((4, 1, TILE, TILE), lambda i: (0, i, 0, 0))] * 5,
        out_specs=pl.BlockSpec((1, 5, 4 * TILE, 2 * TILE), lambda i: (i, 0, 0, 0)),
        cost_estimate=pl.CostEstimate(flops=5 * 10**6, bytes_accessed=10**7, transcendentals=0),
        name="split_kets",
    )(sector, *[k.reshape(4, 4, TILE, TILE) for k in kets])


def pair_kernel(
    sector_ref, region_ref, class_ref, live_ref, out_ref, block_ref, place_ref, left_ref, right_ref,
    start_ref, passed0_ref, passed1_ref, kets_hbm, *refs,
):
    rights_hbm = refs[:9]
    image_ref, kets, arrived, rights, envs, even, odd, middle, *rest = refs[9:]
    outer_even, outer_odd, sems = rest
    sector = sector_ref[0]

    def kets_copy(t):
        return pltpu.make_async_copy(kets_hbm.at[t], kets.at[t], sems.at[t])

    def rights_copy(n):
        return pltpu.make_async_copy(rights_hbm[n], arrived.at[n % 2], sems.at[4 + n % 2])

    for t in range(4):
        kets_copy(t).start()
    for n in range(2):
        rights_copy(n).start()

    @pl.when(region_ref[0] == 0)
    def _():
        def own(w):
            keep = inside(sector + class_shift(class_ref[w]))
            envs[w] = stacked((start_ref[w] * keep).T)

        loop(0, NW, own, 1)

    @pl.when(region_ref[0] != 0)
    def _():
        for first, ref in ((0, passed0_ref), (9, passed1_ref)):
            for n in range(ref.shape[0]):
                envs[first + n] = stacked(ref[n])

    def form(product, t2, w):
        result = folded(dot(kets[t2, class_ref[w]], envs[w]))
        product[pl.ds(4 * w, 4)] = result.reshape(4, TILE, TILE)

    def left(product, t2, s, i):
        v = out_ref[s, i]
        terms = LONG if i < LONG else SHORT
        total = mix(product, 0, block_ref, place_ref, left_ref, v, class_ref[v], s, terms)
        middle[s * 4 * NW + 4 * v + t2] = total

    kets_copy(0).wait()
    loop(0, NW, functools.partial(form, even, 0), 1)
    for n in range(9):
        rights_copy(n).wait()

        def cut(x):
            ups, downs = n // 3, n % 3
            keep = inside(sector + ND * ups + downs + class_shift(class_ref[x]))
            rights[n, x] = jnp.concatenate(split(arrived[n % 2, x] * keep), axis=0)

        loop(0, NW - 1, cut, 4)
        cut(NW - 1)
        if n + 2 < 9:
            rights_copy(n + 2).start()
    for t in range(1, 4):
        kets_copy(t).wait()

    def stage(here, there, t2):
        later = jnp.minimum(t2 + 1, 3)

        def step(s):
            for i in range(NW):
                left(here, t2, s, i)
                if i % 4 == 0:
                    form(there, later, jnp.minimum(5 * s + i // 4, NW - 1))

        loop(0, 4, step, 1)

    def stages(half):
        stage(even, odd, 2 * half)
        stage(odd, even, 2 * half + 1)

    loop(0, 2, stages, 1)

    rows = lax.broadcasted_iota(jnp.int32, (TILE, TILE), 0)
    columns = lax.broadcasted_iota(jnp.int32, (TILE, TILE), 1)
    own = live_ref[0, MAXLEN, sector]

    def place_of(p):
        s1 = p // 4
        s2 = p % 4
        ups = s1 % 2 + s2 % 2
        downs = s1 // 2 + s2 // 2
        return s1, s2, 3 * ups + downs, sector + ND * ups + downs

    def close(outer, p):
        _, s2, step, far = place_of(p)
        lhs = [rights[step, out_ref[s2, i]] for i in range(NW)]
        total = dot(jnp.concatenate(lhs, axis=1), outer[...])
        total = folded(total[:TILE] + total[TILE:]).T
        count = jnp.where(far < NSEC, live_ref[0, MAXLEN, jnp.minimum(far, NSEC - 1)], 0)
        image_ref[p] = jnp.where((rows < own) & (columns < count), total, 0.0)

    def right(outer, p):
        s1, s2, _, _ = place_of(p)
        for i in range(NW):
            x = out_ref[s2, i]
            terms = LONG if i < LONG else SHORT
            total = mix(middle, s1 * 4 * NW, block_ref, place_ref, right_ref, x, class_ref[x], s2, terms)
            high, low = split(total)
            outer[i * TILE : (i + 1) * TILE, :TILE] = high
            outer[i * TILE : (i + 1) * TILE, TILE:] = low

    right(outer_even, 0)

    def right_stages(half):
        p = 2 * half
        close(outer_even, p)
        right(outer_odd, p + 1)
        close(outer_odd, p + 1)
        right(outer_even, jnp.minimum(p + 2, 15))

    loop(0, 8, right_stages, 1)


def pair(scalars, start, passed, kets, rights):
    return pl.pallas_call(
        pair_kernel,
        out_shape=jax.ShapeDtypeStruct((16, TILE, TILE), F32),
        in_specs=[SMEM_SPEC] * 9 + [VMEM_SPEC] * 3 + [HBM_SPEC] * 10,
        out_specs=VMEM_SPEC,
        scratch_shapes=[
            pltpu.VMEM((4, 5, 4 * TILE, 2 * TILE), BF16),
            pltpu.VMEM((2, NW, TILE, TILE), F32),
            pltpu.VMEM((9, NW, 2 * TILE, TILE), BF16),
            pltpu.VMEM((NW, 2 * TILE, 2 * TILE), BF16),
            pltpu.VMEM((4 * NW, TILE, TILE), F32),
            pltpu.VMEM((4 * NW, TILE, TILE), F32),
            pltpu.VMEM((16 * NW, TILE, TILE), F32),
            pltpu.VMEM((NW * TILE, 2 * TILE), BF16),
            pltpu.VMEM((NW * TILE, 2 * TILE), BF16),
            pltpu.SemaphoreType.DMA((6,)),
        ],
        compiler_params=pltpu.CompilerParams(vmem_limit_bytes=60 * 2**20),
        cost_estimate=pl.CostEstimate(flops=20 * 10**9, bytes_accessed=18 * 10**6, transcendentals=0),
        name="pair",
    )(*scalars, start, *passed, kets, *rights)


def turn_kernel(e0, e1, out_ref):
    for first, ref in ((0, e0), (9, e1)):
        for n in range(ref.shape[0]):
            out_ref[first + n] = ref[n].T


def turned(parts):
    return pl.pallas_call(
        turn_kernel,
        out_shape=jax.ShapeDtypeStruct((NW, TILE, TILE), F32),
        in_specs=[VMEM_SPEC] * 2,
        out_specs=VMEM_SPEC,
        cost_estimate=pl.CostEstimate(flops=10**6, bytes_accessed=2228224, transcendentals=0),
        name="turn",
    )(*parts)


def fetch(blocks, offset, axis="block"):
    length = lax.axis_size(axis)
    pairs = [(i, i - offset) for i in range(length) if 0 <= i - offset < length]
    return lax.ppermute(blocks, axis, pairs)


def fetch_next(sector, blocks, above):
    blocks, above = lax.optimization_barrier((blocks, above))
    given = jnp.where(sector[0] % ND == 0, above, blocks)
    pairs = [(i, i // ND * ND + (i - 1) % ND) for i in range(NSEC)]
    return lax.ppermute(given, "block", pairs)


def flat_rule(rule):
    return jnp.pad(rule.reshape(RULE), (0, PADDED - RULE))


def shards(
    env_left,
    env_right,
    site_tensors,
    pair_state,
    mpo_sites,
    mpo_pair,
    channel_class,
    live_rows,
    region_sites,
):
    start = env_left[0, :, 0]
    right = env_right[0, :, 0]
    tensors = site_tensors[0, :, :, 0]
    pairs = pair_state[0, :, 0]
    sector = lax.axis_index("block").astype(jnp.int32).reshape(1)
    region = lax.axis_index("region").astype(jnp.int32).reshape(1)

    near3 = fetch(tensors, ND)
    near4 = fetch(tensors, -ND)
    near1 = fetch(tensors, 1)
    near2 = fetch(tensors, -1)
    near = [tensors, near1, near2, near3, near4]
    rights = {(0, 0): right}
    rights[1, 0] = fetch(right, ND)
    rights[2, 0] = fetch(rights[1, 0], ND)
    rights[0, 1] = fetch_next(sector, right, rights[1, 0])
    rights[1, 1] = fetch_next(sector, rights[1, 0], rights[2, 0])
    rights[2, 1] = fetch(rights[2, 0], 1)
    rights[0, 2] = fetch_next(sector, rights[0, 1], rights[1, 1])
    rights[1, 2] = fetch_next(sector, rights[1, 1], rights[2, 1])
    rights[2, 2] = fetch(rights[2, 1], 1)
    pairs2 = fetch(pairs, -1)
    pairs3 = fetch(pairs, ND)
    pairs4 = fetch(pairs, -ND)
    pairs1 = fetch_next(sector, pairs, pairs3)
    kets = [pairs, pairs1, pairs2, pairs3, pairs4]

    tables = mix_tables(channel_class)
    scalars = (sector, channel_class, live_rows, *tables)
    h0, h1, h2, h3 = site(0, (*scalars, flat_rule(mpo_sites[0, 0])), [start], near)
    below3 = fetch(h3, -1)
    below2 = fetch(h2, -1)
    partial = fetch(h1 + below3, -ND)

    h0, h1, h2, h3, first = site(1, (*scalars, flat_rule(mpo_sites[0, 1])), [h0, below2, partial], near)
    below3 = fetch(h3, -1)
    below2 = fetch(h2, -1)
    upper = h1 + below3
    ket = sector + class_shift(channel_class)
    sectors = jnp.arange(NSEC, dtype=jnp.int32)
    width = jnp.arange(TILE, dtype=jnp.int32)
    count = jnp.where(ket[:, None] == sectors, live_rows[0, 1], 0).sum(-1)
    own = jnp.where(sector == sectors, live_rows[0, 1], 0).sum()
    keep = (width[:, None] < count[:, None, None]) & (width < own)
    parts = []
    passed = []
    for lo, hi in ((0, 9), (9, NW)):
        partial = fetch(upper[lo:hi], -ND)
        second = jnp.where(keep[lo:hi], h0[lo:hi] + below2[lo:hi] + partial, 0.0)
        second = jnp.where(region_sites[0] > 1, second, first[lo:hi])
        parts.append(second)
        passed.append(fetch(second, -1, "region"))

    environment = turned(parts)
    split = split_kets(sector, kets)
    scalars = (sector, region, channel_class, live_rows, *tables, flat_rule(mpo_pair[0, 0]), flat_rule(mpo_pair[0, 1]))
    images = pair(scalars, start, passed, split, [rights[u, d] for u in range(3) for d in range(3)])
    return environment[None, :, None], images[None, :, None]


def solution(mesh):
    in_specs = (
        P("region", None, "block", None, None),
        P("region", None, "block", None, None),
        P("region", None, None, "block", None, None),
        P("region", None, "block", None, None),
        P("region", None, None, None, None, None),
        P("region", None, None, None, None, None),
        P(),
        P("region", None, None),
        P("region"),
    )
    out_specs = (P("region", None, "block", None, None), P("region", None, "block", None, None))
    return jax.shard_map(shards, mesh=mesh, in_specs=in_specs, out_specs=out_specs, check_vma=False)
```

```python
import functools
import jax
import jax.numpy as jnp
from jax import lax
from jax.experimental import pallas as pl
from jax.experimental.pallas import tpu as pltpu
from jax.sharding import PartitionSpec as P

NSEC = 32
TILE = 128
NW = 17
ND = 8
MAXLEN = 2
STATE_STEPS = (0, ND, 1, ND + 1)
CLASS_STEPS = (0, 1, -1, ND, -ND)
LONG = 11
SHORT = 5
RULE = NW * NW * 16
PADDED = RULE + NW * 16
F32 = jnp.float32
BF16 = jnp.bfloat16


def mix_tables(channel_class):
    steps = jnp.array(STATE_STEPS, dtype=jnp.int32)
    shifts = class_shift(channel_class)
    source = (shifts[:, None] + steps[None, :]).reshape(-1)
    goal = (jnp.array(CLASS_STEPS, dtype=jnp.int32)[:, None] + steps[None, :]).reshape(-1)
    order = jnp.arange(4 * NW, dtype=jnp.int32)
    allowed = goal[:, None] == source[None, :]
    earlier = allowed[:, None, :] & (order[None, :] < order[:, None])
    rank = earlier.astype(jnp.int32).sum(-1)
    term = allowed[:, None, :] & (rank[:, None, :] == jnp.arange(LONG, dtype=jnp.int32)[:, None])
    block = jnp.where(term, order, 0).sum(-1)
    place = jnp.where(term, (order // 4) * (NW * 16) + order % 4 - RULE, 0).sum(-1) + RULE

    down = (jnp.arange(4) // 2)[:, None]
    up = (jnp.arange(4) % 2)[:, None]
    kind = channel_class[None, :]
    three = (
        (kind == 0)
        | ((kind == 1) & (down == 0))
        | ((kind == 2) & (down == 1))
        | ((kind == 3) & (up == 0))
        | ((kind == 4) & (up == 1))
    )
    channels = jnp.arange(NW, dtype=jnp.int32)
    key = jnp.where(three, 0, NW) + channels[None, :]
    position = (key[:, None, :] < key[:, :, None]).astype(jnp.int32).sum(-1)
    out = jnp.where(position[:, None, :] == channels[:, None], channels, 0).sum(-1)
    return out, block, place


def class_shift(kind):
    return jnp.where(kind == 1, 1, jnp.where(kind == 2, -1, jnp.where(kind == 3, ND, jnp.where(kind == 4, -ND, 0))))


def inside(sector):
    return ((sector >= 0) & (sector < NSEC)).astype(F32)


def split(x):
    high = x.astype(BF16)
    return high, (x - high.astype(F32)).astype(BF16)


def mix(blocks, base, block_ref, place_ref, rule_ref, v, kind, s, terms):
    row = 4 * kind + s
    shift = 16 * v + 4 * s
    total = None
    for k in range(terms):
        term = blocks[base + block_ref[row, k]] * rule_ref[place_ref[row, k] + shift]
        total = term if total is None else total + term
    return total


def stacked(x):
    row = jnp.concatenate(split(x), axis=1)
    return jnp.concatenate([row, row], axis=0)


def folded(x):
    return x[:, :TILE] + x[:, TILE:]


def dot(a, b):
    return jnp.dot(a, b, preferred_element_type=F32)


def loop(start, stop, body, unroll):
    lax.fori_loop(start, stop, lambda i, c: (body(i), c)[1], 0, unroll=unroll)


def site_kernel(
    number, sector_ref, class_ref, live_ref, out_ref, block_ref, place_ref, rule_ref, *refs
):
    if number == 0:
        env_ref, *refs = refs
    else:
        low_ref, below_ref, above_ref, *refs = refs
    kets_refs, refs = refs[:5], refs[5:]
    closed_refs, refs = refs[:4], refs[4:]
    if number > 0:
        first_ref, *refs = refs
    kets, product, bras, _ = refs
    sector = sector_ref[0]

    for c, ref in enumerate(kets_refs):
        for t in range(4):
            keep = inside(sector + CLASS_STEPS[c] + STATE_STEPS[t])
            high, low = split(ref[0, t].T * keep)
            kets[c, t * TILE : (t + 1) * TILE, :TILE] = high
            kets[c, t * TILE : (t + 1) * TILE, TILE:] = low
    for s in range(4):
        bras[s] = stacked(kets_refs[0][0, s] * inside(sector + STATE_STEPS[s]))

    rows = lax.broadcasted_iota(jnp.int32, (TILE, TILE), 1)
    columns = lax.broadcasted_iota(jnp.int32, (TILE, TILE), 0)

    def environment(w):
        ket = sector + class_shift(class_ref[w])
        keep = inside(ket)
        if number == 0:
            return (env_ref[w] * keep).T
        count = jnp.where(keep > 0, live_ref[0, number - 1, jnp.clip(ket, 0, NSEC - 1)], 0)
        own = live_ref[0, number - 1, sector]
        total = low_ref[w] + below_ref[w] + above_ref[w]
        total = jnp.where((rows < own) & (columns < count), total, 0.0)
        first_ref[w] = total
        return total

    def form(w):
        result = folded(dot(kets[class_ref[w]], stacked(environment(w))))
        product[pl.ds(4 * w, 4)] = result.reshape(4, TILE, TILE)

    loop(0, NW, form, 1)

    for s in (3, 2, 1, 0):

        def close(terms, i):
            v = out_ref[s, i]
            total = mix(product, 0, block_ref, place_ref, rule_ref, v, class_ref[v], s, terms)
            result = folded(dot(jnp.concatenate(split(total), axis=1), bras[s]))
            closed_refs[s][v] = result

        loop(0, LONG, functools.partial(close, LONG), UNROLL_LONG)
        loop(LONG, NW, functools.partial(close, SHORT), UNROLL_SHORT)


UNROLL_LONG = 11
UNROLL_SHORT = 6
SMEM_SPEC = pl.BlockSpec(memory_space=pltpu.SMEM)
VMEM_SPEC = pl.BlockSpec(memory_space=pltpu.VMEM)
HBM_SPEC = pl.BlockSpec(memory_space=pl.ANY)


def site(number, scalars, envs, kets):
    block = jax.ShapeDtypeStruct((NW, TILE, TILE), F32)
    count = 4 if number == 0 else 5
    ket_spec = pl.BlockSpec((1, 4, TILE, TILE), lambda i: (number, 0, 0, 0))
    return pl.pallas_call(
        functools.partial(site_kernel, number),
        grid=(1,),
        out_shape=[block] * count,
        in_specs=[SMEM_SPEC] * 7 + [VMEM_SPEC] * len(envs) + [ket_spec] * 5,
        out_specs=[VMEM_SPEC] * count,
        scratch_shapes=[
            pltpu.VMEM((5, 4 * TILE, 2 * TILE), BF16),
            pltpu.VMEM((4 * NW, TILE, TILE), F32),
            pltpu.VMEM((4, 2 * TILE, 2 * TILE), BF16),
            pltpu.VMEM((2 * TILE, 2 * TILE), BF16),
        ],
        compiler_params=pltpu.CompilerParams(vmem_limit_bytes=60 * 2**20),
        cost_estimate=pl.CostEstimate(flops=4 * 10**9, bytes_accessed=10**7, transcendentals=0),
    )(*scalars, *envs, *kets)


def kets_kernel(sector_ref, k0, k1, k2, k3, k4, out_ref):
    t2 = pl.program_id(0)
    step2 = (t2 % 2) * ND + t2 // 2
    for c, ref in enumerate((k0, k1, k2, k3, k4)):
        for t1 in range(4):
            keep = inside(sector_ref[0] + CLASS_STEPS[c] + STATE_STEPS[t1] + step2)
            high, low = split(ref[t1, 0].T * keep)
            out_ref[0, c, t1 * TILE : (t1 + 1) * TILE, :TILE] = high
            out_ref[0, c, t1 * TILE : (t1 + 1) * TILE, TILE:] = low


def split_kets(sector, kets):
    return pl.pallas_call(
        kets_kernel,
        grid=(4,),
        out_shape=jax.ShapeDtypeStruct((4, 5, 4 * TILE, 2 * TILE), BF16),
        in_specs=[SMEM_SPEC] + [pl.BlockSpec((4, 1, TILE, TILE), lambda i: (0, i, 0, 0))] * 5,
        out_specs=pl.BlockSpec((1, 5, 4 * TILE, 2 * TILE), lambda i: (i, 0, 0, 0)),
        cost_estimate=pl.CostEstimate(flops=5 * 10**6, bytes_accessed=10**7, transcendentals=0),
        name="split_kets",
    )(sector, *[k.reshape(4, 4, TILE, TILE) for k in kets])


def pair_kernel(
    sector_ref, region_ref, class_ref, live_ref, out_ref, block_ref, place_ref, left_ref, right_ref,
    start_ref, passed0_ref, passed1_ref, kets_hbm, *refs,
):
    rights_hbm = refs[:9]
    image_ref, kets, arrived, rights, envs, even, odd, middle, *rest = refs[9:]
    outer_even, outer_odd, sems = rest
    sector = sector_ref[0]

    def kets_copy(t):
        return pltpu.make_async_copy(kets_hbm.at[t], kets.at[t], sems.at[t])

    def rights_copy(n):
        return pltpu.make_async_copy(rights_hbm[n], arrived.at[n % 2], sems.at[4 + n % 2])

    for t in range(4):
        kets_copy(t).start()
    for n in range(2):
        rights_copy(n).start()

    @pl.when(region_ref[0] == 0)
    def _():
        def own(w):
            keep = inside(sector + class_shift(class_ref[w]))
            envs[w] = stacked((start_ref[w] * keep).T)

        loop(0, NW, own, 1)

    @pl.when(region_ref[0] != 0)
    def _():
        for first, ref in ((0, passed0_ref), (9, passed1_ref)):
            for n in range(ref.shape[0]):
                envs[first + n] = stacked(ref[n])

    def form(product, t2, w):
        result = folded(dot(kets[t2, class_ref[w]], envs[w]))
        product[pl.ds(4 * w, 4)] = result.reshape(4, TILE, TILE)

    def left(product, t2, s, i):
        v = out_ref[s, i]
        terms = LONG if i < LONG else SHORT
        total = mix(product, 0, block_ref, place_ref, left_ref, v, class_ref[v], s, terms)
        middle[s * 4 * NW + 4 * v + t2] = total

    kets_copy(0).wait()
    loop(0, NW, functools.partial(form, even, 0), 1)
    for n in range(9):
        rights_copy(n).wait()

        def cut(x):
            ups, downs = n // 3, n % 3
            keep = inside(sector + ND * ups + downs + class_shift(class_ref[x]))
            rights[n, x] = jnp.concatenate(split(arrived[n % 2, x] * keep), axis=0)

        loop(0, NW - 1, cut, 4)
        cut(NW - 1)
        if n + 2 < 9:
            rights_copy(n + 2).start()
    for t in range(1, 4):
        kets_copy(t).wait()

    def stage(here, there, t2):
        later = jnp.minimum(t2 + 1, 3)

        def step(s):
            for i in range(NW):
                left(here, t2, s, i)
                if i % 4 == 0:
                    form(there, later, jnp.minimum(5 * s + i // 4, NW - 1))

        loop(0, 4, step, 1)

    def stages(half):
        stage(even, odd, 2 * half)
        stage(odd, even, 2 * half + 1)

    loop(0, 2, stages, 1)

    rows = lax.broadcasted_iota(jnp.int32, (TILE, TILE), 0)
    columns = lax.broadcasted_iota(jnp.int32, (TILE, TILE), 1)
    own = live_ref[0, MAXLEN, sector]

    def place_of(p):
        s1 = p // 4
        s2 = p % 4
        ups = s1 % 2 + s2 % 2
        downs = s1 // 2 + s2 // 2
        return s1, s2, 3 * ups + downs, sector + ND * ups + downs

    def close(outer, p):
        _, s2, step, far = place_of(p)
        lhs = [rights[step, out_ref[s2, i]] for i in range(NW)]
        total = dot(jnp.concatenate(lhs, axis=1), outer[...])
        total = folded(total[:TILE] + total[TILE:]).T
        count = jnp.where(far < NSEC, live_ref[0, MAXLEN, jnp.minimum(far, NSEC - 1)], 0)
        image_ref[p] = jnp.where((rows < own) & (columns < count), total, 0.0)

    def right(outer, p):
        s1, s2, _, _ = place_of(p)
        for i in range(NW):
            x = out_ref[s2, i]
            terms = LONG if i < LONG else SHORT
            total = mix(middle, s1 * 4 * NW, block_ref, place_ref, right_ref, x, class_ref[x], s2, terms)
            high, low = split(total)
            outer[i * TILE : (i + 1) * TILE, :TILE] = high
            outer[i * TILE : (i + 1) * TILE, TILE:] = low

    right(outer_even, 0)

    def right_stages(half):
        p = 2 * half
        close(outer_even, p)
        right(outer_odd, p + 1)
        close(outer_odd, p + 1)
        right(outer_even, jnp.minimum(p + 2, 15))

    loop(0, 8, right_stages, 1)


def pair(scalars, start, passed, kets, rights):
    return pl.pallas_call(
        pair_kernel,
        out_shape=jax.ShapeDtypeStruct((16, TILE, TILE), F32),
        in_specs=[SMEM_SPEC] * 9 + [VMEM_SPEC] * 3 + [HBM_SPEC] * 10,
        out_specs=VMEM_SPEC,
        scratch_shapes=[
            pltpu.VMEM((4, 5, 4 * TILE, 2 * TILE), BF16),
            pltpu.VMEM((2, NW, TILE, TILE), F32),
            pltpu.VMEM((9, NW, 2 * TILE, TILE), BF16),
            pltpu.VMEM((NW, 2 * TILE, 2 * TILE), BF16),
            pltpu.VMEM((4 * NW, TILE, TILE), F32),
            pltpu.VMEM((4 * NW, TILE, TILE), F32),
            pltpu.VMEM((16 * NW, TILE, TILE), F32),
            pltpu.VMEM((NW * TILE, 2 * TILE), BF16),
            pltpu.VMEM((NW * TILE, 2 * TILE), BF16),
            pltpu.SemaphoreType.DMA((6,)),
        ],
        compiler_params=pltpu.CompilerParams(vmem_limit_bytes=60 * 2**20),
        cost_estimate=pl.CostEstimate(flops=20 * 10**9, bytes_accessed=18 * 10**6, transcendentals=0),
        name="pair",
    )(*scalars, start, *passed, kets, *rights)


def turn_kernel(e0, e1, out_ref):
    for first, ref in ((0, e0), (9, e1)):
        for n in range(ref.shape[0]):
            out_ref[first + n] = ref[n].T


def turned(parts):
    return pl.pallas_call(
        turn_kernel,
        out_shape=jax.ShapeDtypeStruct((NW, TILE, TILE), F32),
        in_specs=[VMEM_SPEC] * 2,
        out_specs=VMEM_SPEC,
        cost_estimate=pl.CostEstimate(flops=10**6, bytes_accessed=2228224, transcendentals=0),
        name="turn",
    )(*parts)


def fetch(blocks, offset, axis="block"):
    length = lax.axis_size(axis)
    pairs = [(i, i - offset) for i in range(length) if 0 <= i - offset < length]
    return lax.ppermute(blocks, axis, pairs)


def fetch_next(sector, blocks, above):
    blocks, above = lax.optimization_barrier((blocks, above))
    given = jnp.where(sector[0] % ND == 0, above, blocks)
    pairs = [(i, i // ND * ND + (i - 1) % ND) for i in range(NSEC)]
    return lax.ppermute(given, "block", pairs)


def flat_rule(rule):
    return jnp.pad(rule.reshape(RULE), (0, PADDED - RULE))


def shards(
    env_left,
    env_right,
    site_tensors,
    pair_state,
    mpo_sites,
    mpo_pair,
    channel_class,
    live_rows,
    region_sites,
):
    start = env_left[0, :, 0]
    right = env_right[0, :, 0]
    tensors = site_tensors[0, :, :, 0]
    pairs = pair_state[0, :, 0]
    sector = lax.axis_index("block").astype(jnp.int32).reshape(1)
    region = lax.axis_index("region").astype(jnp.int32).reshape(1)

    near3 = fetch(tensors, ND)
    near4 = fetch(tensors, -ND)
    near1 = fetch(tensors, 1)
    near2 = fetch(tensors, -1)
    near = [tensors, near1, near2, near3, near4]
    rights = {(0, 0): right}
    rights[1, 0] = fetch(right, ND)
    rights[2, 0] = fetch(rights[1, 0], ND)
    rights[0, 1] = fetch_next(sector, right, rights[1, 0])
    rights[1, 1] = fetch_next(sector, rights[1, 0], rights[2, 0])
    rights[2, 1] = fetch(rights[2, 0], 1)
    rights[0, 2] = fetch_next(sector, rights[0, 1], rights[1, 1])
    rights[1, 2] = fetch_next(sector, rights[1, 1], rights[2, 1])
    rights[2, 2] = fetch(rights[2, 1], 1)
    pairs2 = fetch(pairs, -1)
    pairs3 = fetch(pairs, ND)
    pairs4 = fetch(pairs, -ND)
    pairs1 = fetch_next(sector, pairs, pairs3)
    kets = [pairs, pairs1, pairs2, pairs3, pairs4]

    tables = mix_tables(channel_class)
    scalars = (sector, channel_class, live_rows, *tables)
    h0, h1, h2, h3 = site(0, (*scalars, flat_rule(mpo_sites[0, 0])), [start], near)
    below3 = fetch(h3, -1)
    below2 = fetch(h2, -1)
    partial = fetch(h1 + below3, -ND)

    h0, h1, h2, h3, first = site(1, (*scalars, flat_rule(mpo_sites[0, 1])), [h0, below2, partial], near)
    below3 = fetch(h3, -1)
    below2 = fetch(h2, -1)
    upper = h1 + below3
    ket = sector + class_shift(channel_class)
    sectors = jnp.arange(NSEC, dtype=jnp.int32)
    width = jnp.arange(TILE, dtype=jnp.int32)
    count = jnp.where(ket[:, None] == sectors, live_rows[0, 1], 0).sum(-1)
    own = jnp.where(sector == sectors, live_rows[0, 1], 0).sum()
    keep = (width[:, None] < count[:, None, None]) & (width < own)
    parts = []
    passed = []
    for n, (lo, hi) in enumerate(((0, 9), (9, NW))):
        partial = fetch(upper[lo:hi], -ND)
        second = jnp.where(keep[lo:hi], h0[lo:hi] + below2[lo:hi] + partial, 0.0)
        second = jnp.where(region_sites[0] > 1, second, first[lo:hi])
        if n == 0:
            split = split_kets(sector, kets)
            rules = (flat_rule(mpo_pair[0, 0]), flat_rule(mpo_pair[0, 1]))
            second, split, *rules = lax.optimization_barrier((second, split, *rules))
        parts.append(second)
        passed.append(fetch(second, -1, "region"))

    environment = turned(parts)
    scalars = (sector, region, channel_class, live_rows, *tables, *rules)
    images = pair(scalars, start, passed, split, [rights[u, d] for u in range(3) for d in range(3)])
    return environment[None, :, None], images[None, :, None]


def solution(mesh):
    in_specs = (
        P("region", None, "block", None, None),
        P("region", None, "block", None, None),
        P("region", None, None, "block", None, None),
        P("region", None, "block", None, None),
        P("region", None, None, None, None, None),
        P("region", None, None, None, None, None),
        P(),
        P("region", None, None),
        P("region"),
    )
    out_specs = (P("region", None, "block", None, None), P("region", None, "block", None, None))
    return jax.shard_map(shards, mesh=mesh, in_specs=in_specs, out_specs=out_specs, check_vma=False)
```

```python
import functools
import jax
import jax.numpy as jnp
from jax import lax
from jax.experimental import pallas as pl
from jax.experimental.pallas import tpu as pltpu
from jax.sharding import PartitionSpec as P

NSEC = 32
TILE = 128
NW = 17
ND = 8
MAXLEN = 2
STATE_STEPS = (0, ND, 1, ND + 1)
CLASS_STEPS = (0, 1, -1, ND, -ND)
LONG = 11
SHORT = 5
RULE = NW * NW * 16
PADDED = RULE + NW * 16
F32 = jnp.float32
BF16 = jnp.bfloat16


def mix_tables(channel_class):
    steps = jnp.array(STATE_STEPS, dtype=jnp.int32)
    shifts = class_shift(channel_class)
    source = (shifts[:, None] + steps[None, :]).reshape(-1)
    goal = (jnp.array(CLASS_STEPS, dtype=jnp.int32)[:, None] + steps[None, :]).reshape(-1)
    order = jnp.arange(4 * NW, dtype=jnp.int32)
    allowed = goal[:, None] == source[None, :]
    earlier = allowed[:, None, :] & (order[None, :] < order[:, None])
    rank = earlier.astype(jnp.int32).sum(-1)
    term = allowed[:, None, :] & (rank[:, None, :] == jnp.arange(LONG, dtype=jnp.int32)[:, None])
    block = jnp.where(term, order, 0).sum(-1)
    place = jnp.where(term, (order // 4) * (NW * 16) + order % 4 - RULE, 0).sum(-1) + RULE

    down = (jnp.arange(4) // 2)[:, None]
    up = (jnp.arange(4) % 2)[:, None]
    kind = channel_class[None, :]
    three = (
        (kind == 0)
        | ((kind == 1) & (down == 0))
        | ((kind == 2) & (down == 1))
        | ((kind == 3) & (up == 0))
        | ((kind == 4) & (up == 1))
    )
    channels = jnp.arange(NW, dtype=jnp.int32)
    key = jnp.where(three, 0, NW) + channels[None, :]
    position = (key[:, None, :] < key[:, :, None]).astype(jnp.int32).sum(-1)
    out = jnp.where(position[:, None, :] == channels[:, None], channels, 0).sum(-1)
    return out, block, place


def class_shift(kind):
    return jnp.where(kind == 1, 1, jnp.where(kind == 2, -1, jnp.where(kind == 3, ND, jnp.where(kind == 4, -ND, 0))))


def inside(sector):
    return ((sector >= 0) & (sector < NSEC)).astype(F32)


def split(x):
    high = x.astype(BF16)
    return high, (x - high.astype(F32)).astype(BF16)


def mix(blocks, base, block_ref, place_ref, rule_ref, v, kind, s, terms):
    row = 4 * kind + s
    shift = 16 * v + 4 * s
    total = None
    for k in range(terms):
        term = blocks[base + block_ref[row, k]] * rule_ref[place_ref[row, k] + shift]
        total = term if total is None else total + term
    return total


def stacked(x):
    row = jnp.concatenate(split(x), axis=1)
    return jnp.concatenate([row, row], axis=0)


def folded(x):
    return x[:, :TILE] + x[:, TILE:]


def dot(a, b):
    return jnp.dot(a, b, preferred_element_type=F32)


def loop(start, stop, body, unroll):
    lax.fori_loop(start, stop, lambda i, c: (body(i), c)[1], 0, unroll=unroll)


def site_kernel(
    number, sector_ref, class_ref, live_ref, out_ref, block_ref, place_ref, rule_ref, *refs
):
    if number == 0:
        env_ref, *refs = refs
    else:
        low_ref, *below_refs = refs[:3]
        above_refs, refs = refs[3:5], refs[5:]
    kets_refs, refs = refs[:5], refs[5:]
    closed_hbm, refs = refs[:6], refs[6:]
    if number > 0:
        first_ref, *refs = refs
    kets, product, bras, closed, sems = refs
    sector = sector_ref[0]

    for c, ref in enumerate(kets_refs):
        for t in range(4):
            keep = inside(sector + CLASS_STEPS[c] + STATE_STEPS[t])
            high, low = split(ref[0, t].T * keep)
            kets[c, t * TILE : (t + 1) * TILE, :TILE] = high
            kets[c, t * TILE : (t + 1) * TILE, TILE:] = low
    for s in range(4):
        bras[s] = stacked(kets_refs[0][0, s] * inside(sector + STATE_STEPS[s]))

    rows = lax.broadcasted_iota(jnp.int32, (TILE, TILE), 1)
    columns = lax.broadcasted_iota(jnp.int32, (TILE, TILE), 0)

    def environment(w, n):
        ket = sector + class_shift(class_ref[w])
        keep = inside(ket)
        if number == 0:
            return (env_ref[w] * keep).T
        count = jnp.where(keep > 0, live_ref[0, number - 1, jnp.clip(ket, 0, NSEC - 1)], 0)
        own = live_ref[0, number - 1, sector]
        below = jnp.where(sector % ND == 0, 0.0, below_refs[n][w - CHUNKS[n][0]])
        total = low_ref[w] + below + above_refs[n][w - CHUNKS[n][0]]
        total = jnp.where((rows < own) & (columns < count), total, 0.0)
        first_ref[w] = total
        return total

    def form(n, w):
        result = folded(dot(kets[class_ref[w]], stacked(environment(w, n))))
        product[pl.ds(4 * w, 4)] = result.reshape(4, TILE, TILE)

    for n, (start, stop) in enumerate(CHUNKS):
        loop(start, stop, functools.partial(form, n), 1)

    copies = []
    for s in (3, 2, 1, 0):

        def close(terms, i):
            v = out_ref[s, i]
            total = mix(product, 0, block_ref, place_ref, rule_ref, v, class_ref[v], s, terms)
            result = folded(dot(jnp.concatenate(split(total), axis=1), bras[s]))
            closed[s, v] = result

        loop(0, LONG, functools.partial(close, LONG), UNROLL_LONG)
        loop(LONG, NW, functools.partial(close, SHORT), UNROLL_SHORT)
        for start, stop in CHUNKS if s >= 2 else ((0, NW),):
            n = len(copies)
            copy = pltpu.make_async_copy(
                closed.at[s, pl.ds(start, stop - start)], closed_hbm[n], sems.at[n]
            )
            copy.start()
            copies.append(copy)
    for copy in copies:
        copy.wait()


CHUNKS = ((0, 9), (9, NW))
UNROLL_LONG = 11
UNROLL_SHORT = 6
SMEM_SPEC = pl.BlockSpec(memory_space=pltpu.SMEM)
VMEM_SPEC = pl.BlockSpec(memory_space=pltpu.VMEM)
HBM_SPEC = pl.BlockSpec(memory_space=pl.ANY)


def site(number, scalars, envs, kets):
    sizes = [stop - start for start, stop in CHUNKS]
    blocks = [jax.ShapeDtypeStruct((n, TILE, TILE), F32) for n in (*sizes, *sizes, NW, NW, NW)]
    count = 6 if number == 0 else 7
    ket_spec = pl.BlockSpec((1, 4, TILE, TILE), lambda i: (number, 0, 0, 0))
    return pl.pallas_call(
        functools.partial(site_kernel, number),
        grid=(1,),
        out_shape=blocks[:count],
        in_specs=[SMEM_SPEC] * 7 + [VMEM_SPEC] * len(envs) + [ket_spec] * 5,
        out_specs=([HBM_SPEC] * 6 + [VMEM_SPEC])[:count],
        scratch_shapes=[
            pltpu.VMEM((5, 4 * TILE, 2 * TILE), BF16),
            pltpu.VMEM((4 * NW, TILE, TILE), F32),
            pltpu.VMEM((4, 2 * TILE, 2 * TILE), BF16),
            pltpu.VMEM((4, NW, TILE, TILE), F32),
            pltpu.SemaphoreType.DMA((6,)),
        ],
        compiler_params=pltpu.CompilerParams(vmem_limit_bytes=60 * 2**20),
        cost_estimate=pl.CostEstimate(flops=4 * 10**9, bytes_accessed=10**7, transcendentals=0),
    )(*scalars, *envs, *kets)


def kets_kernel(sector_ref, k0, k1, k2, k3, k4, out_ref):
    t2 = pl.program_id(0)
    step2 = (t2 % 2) * ND + t2 // 2
    for c, ref in enumerate((k0, k1, k2, k3, k4)):
        for t1 in range(4):
            keep = inside(sector_ref[0] + CLASS_STEPS[c] + STATE_STEPS[t1] + step2)
            high, low = split(ref[t1, 0].T * keep)
            out_ref[0, c, t1 * TILE : (t1 + 1) * TILE, :TILE] = high
            out_ref[0, c, t1 * TILE : (t1 + 1) * TILE, TILE:] = low


def split_kets(sector, kets):
    return pl.pallas_call(
        kets_kernel,
        grid=(4,),
        out_shape=jax.ShapeDtypeStruct((4, 5, 4 * TILE, 2 * TILE), BF16),
        in_specs=[SMEM_SPEC] + [pl.BlockSpec((4, 1, TILE, TILE), lambda i: (0, i, 0, 0))] * 5,
        out_specs=pl.BlockSpec((1, 5, 4 * TILE, 2 * TILE), lambda i: (i, 0, 0, 0)),
        cost_estimate=pl.CostEstimate(flops=5 * 10**6, bytes_accessed=10**7, transcendentals=0),
        name="split_kets",
    )(sector, *[k.reshape(4, 4, TILE, TILE) for k in kets])


def pair_kernel(
    sector_ref, region_ref, class_ref, live_ref, out_ref, block_ref, place_ref, left_ref, right_ref,
    start_ref, passed0_ref, passed1_ref, kets_hbm, *refs,
):
    rights_hbm = refs[:9]
    image_ref, kets, arrived, rights, envs, even, odd, middle, *rest = refs[9:]
    outer_even, outer_odd, sems = rest
    sector = sector_ref[0]

    def kets_copy(t):
        return pltpu.make_async_copy(kets_hbm.at[t], kets.at[t], sems.at[t])

    def rights_copy(n):
        return pltpu.make_async_copy(rights_hbm[n], arrived.at[n % 2], sems.at[4 + n % 2])

    for t in range(4):
        kets_copy(t).start()
    for n in range(2):
        rights_copy(n).start()

    @pl.when(region_ref[0] == 0)
    def _():
        def own(w):
            keep = inside(sector + class_shift(class_ref[w]))
            envs[w] = stacked((start_ref[w] * keep).T)

        loop(0, NW, own, 1)

    @pl.when(region_ref[0] != 0)
    def _():
        for first, ref in ((0, passed0_ref), (9, passed1_ref)):
            for n in range(ref.shape[0]):
                envs[first + n] = stacked(ref[n])

    def form(product, t2, w):
        result = folded(dot(kets[t2, class_ref[w]], envs[w]))
        product[pl.ds(4 * w, 4)] = result.reshape(4, TILE, TILE)

    def left(product, t2, s, i):
        v = out_ref[s, i]
        terms = LONG if i < LONG else SHORT
        total = mix(product, 0, block_ref, place_ref, left_ref, v, class_ref[v], s, terms)
        middle[s * 4 * NW + 4 * v + t2] = total

    kets_copy(0).wait()
    loop(0, NW, functools.partial(form, even, 0), 1)
    for n in range(9):
        rights_copy(n).wait()

        def cut(x):
            ups, downs = n // 3, n % 3
            keep = inside(sector + ND * ups + downs + class_shift(class_ref[x]))
            rights[n, x] = jnp.concatenate(split(arrived[n % 2, x] * keep), axis=0)

        loop(0, NW - 1, cut, 4)
        cut(NW - 1)
        if n + 2 < 9:
            rights_copy(n + 2).start()
    for t in range(1, 4):
        kets_copy(t).wait()

    def stage(here, there, t2):
        later = jnp.minimum(t2 + 1, 3)

        def step(s):
            for i in range(NW):
                left(here, t2, s, i)
                if i % 4 == 0:
                    form(there, later, jnp.minimum(5 * s + i // 4, NW - 1))

        loop(0, 4, step, 1)

    def stages(half):
        stage(even, odd, 2 * half)
        stage(odd, even, 2 * half + 1)

    loop(0, 2, stages, 1)

    rows = lax.broadcasted_iota(jnp.int32, (TILE, TILE), 0)
    columns = lax.broadcasted_iota(jnp.int32, (TILE, TILE), 1)
    own = live_ref[0, MAXLEN, sector]

    def place_of(p):
        s1 = p // 4
        s2 = p % 4
        ups = s1 % 2 + s2 % 2
        downs = s1 // 2 + s2 // 2
        return s1, s2, 3 * ups + downs, sector + ND * ups + downs

    def close(outer, p):
        _, s2, step, far = place_of(p)
        lhs = [rights[step, out_ref[s2, i]] for i in range(NW)]
        total = dot(jnp.concatenate(lhs, axis=1), outer[...])
        total = folded(total[:TILE] + total[TILE:]).T
        count = jnp.where(far < NSEC, live_ref[0, MAXLEN, jnp.minimum(far, NSEC - 1)], 0)
        image_ref[p] = jnp.where((rows < own) & (columns < count), total, 0.0)

    def right(outer, p):
        s1, s2, _, _ = place_of(p)
        for i in range(NW):
            x = out_ref[s2, i]
            terms = LONG if i < LONG else SHORT
            total = mix(middle, s1 * 4 * NW, block_ref, place_ref, right_ref, x, class_ref[x], s2, terms)
            high, low = split(total)
            outer[i * TILE : (i + 1) * TILE, :TILE] = high
            outer[i * TILE : (i + 1) * TILE, TILE:] = low

    right(outer_even, 0)

    def right_stages(half):
        p = 2 * half
        close(outer_even, p)
        right(outer_odd, p + 1)
        close(outer_odd, p + 1)
        right(outer_even, jnp.minimum(p + 2, 15))

    loop(0, 8, right_stages, 1)


def pair(scalars, start, passed, kets, rights):
    return pl.pallas_call(
        pair_kernel,
        out_shape=jax.ShapeDtypeStruct((16, TILE, TILE), F32),
        in_specs=[SMEM_SPEC] * 9 + [VMEM_SPEC] * 3 + [HBM_SPEC] * 10,
        out_specs=VMEM_SPEC,
        scratch_shapes=[
            pltpu.VMEM((4, 5, 4 * TILE, 2 * TILE), BF16),
            pltpu.VMEM((2, NW, TILE, TILE), F32),
            pltpu.VMEM((9, NW, 2 * TILE, TILE), BF16),
            pltpu.VMEM((NW, 2 * TILE, 2 * TILE), BF16),
            pltpu.VMEM((4 * NW, TILE, TILE), F32),
            pltpu.VMEM((4 * NW, TILE, TILE), F32),
            pltpu.VMEM((16 * NW, TILE, TILE), F32),
            pltpu.VMEM((NW * TILE, 2 * TILE), BF16),
            pltpu.VMEM((NW * TILE, 2 * TILE), BF16),
            pltpu.SemaphoreType.DMA((6,)),
        ],
        compiler_params=pltpu.CompilerParams(vmem_limit_bytes=60 * 2**20),
        cost_estimate=pl.CostEstimate(flops=20 * 10**9, bytes_accessed=18 * 10**6, transcendentals=0),
        name="pair",
    )(*scalars, start, *passed, kets, *rights)


def turn_kernel(e0, e1, out_ref):
    for first, ref in ((0, e0), (9, e1)):
        for n in range(ref.shape[0]):
            out_ref[first + n] = ref[n].T


def turned(parts):
    return pl.pallas_call(
        turn_kernel,
        out_shape=jax.ShapeDtypeStruct((NW, TILE, TILE), F32),
        in_specs=[VMEM_SPEC] * 2,
        out_specs=VMEM_SPEC,
        cost_estimate=pl.CostEstimate(flops=10**6, bytes_accessed=2228224, transcendentals=0),
        name="turn",
    )(*parts)


def fetch(blocks, offset, axis="block"):
    length = lax.axis_size(axis)
    pairs = [(i, i - offset) for i in range(length) if 0 <= i - offset < length]
    return lax.ppermute(blocks, axis, pairs)


def fetch_next(sector, blocks, above):
    blocks, above = lax.optimization_barrier((blocks, above))
    given = jnp.where(sector[0] % ND == 0, above, blocks)
    pairs = [(i, i // ND * ND + (i - 1) % ND) for i in range(NSEC)]
    return lax.ppermute(given, "block", pairs)


def fetch_before(blocks):
    pairs = [(i, i // ND * ND + (i + 1) % ND) for i in range(NSEC)]
    return lax.ppermute(blocks, "block", pairs)


def moved(sector, h1, threes, twos):
    below = []
    above = []
    for n, (lo, hi) in enumerate(CHUNKS):
        three = fetch(threes[n], -1)
        two = fetch_before(twos[n])
        upper = h1[lo:hi] + three + jnp.where(sector[0] % ND == 0, two, 0.0)
        below.append(two)
        above.append(fetch(upper, -ND))
    return below, above


def flat_rule(rule):
    return jnp.pad(rule.reshape(RULE), (0, PADDED - RULE))


def shards(
    env_left,
    env_right,
    site_tensors,
    pair_state,
    mpo_sites,
    mpo_pair,
    channel_class,
    live_rows,
    region_sites,
):
    start = env_left[0, :, 0]
    right = env_right[0, :, 0]
    tensors = site_tensors[0, :, :, 0]
    pairs = pair_state[0, :, 0]
    sector = lax.axis_index("block").astype(jnp.int32).reshape(1)
    region = lax.axis_index("region").astype(jnp.int32).reshape(1)

    near3 = fetch(tensors, ND)
    near4 = fetch(tensors, -ND)
    near1 = fetch(tensors, 1)
    near2 = fetch(tensors, -1)
    near = [tensors, near1, near2, near3, near4]
    rights = {(0, 0): right}
    rights[1, 0] = fetch(right, ND)
    rights[2, 0] = fetch(rights[1, 0], ND)
    rights[0, 1] = fetch_next(sector, right, rights[1, 0])
    rights[1, 1] = fetch_next(sector, rights[1, 0], rights[2, 0])
    rights[2, 1] = fetch(rights[2, 0], 1)
    rights[0, 2] = fetch_next(sector, rights[0, 1], rights[1, 1])
    rights[1, 2] = fetch_next(sector, rights[1, 1], rights[2, 1])
    rights[2, 2] = fetch(rights[2, 1], 1)
    pairs2 = fetch(pairs, -1)
    pairs3 = fetch(pairs, ND)
    pairs4 = fetch(pairs, -ND)
    pairs1 = fetch_next(sector, pairs, pairs3)
    kets = [pairs, pairs1, pairs2, pairs3, pairs4]

    tables = mix_tables(channel_class)
    scalars = (sector, channel_class, live_rows, *tables)
    *parts, h1, h0 = site(0, (*scalars, flat_rule(mpo_sites[0, 0])), [start], near)
    below, above = moved(sector, h1, parts[:2], parts[2:])
    second_rule, below[1] = lax.optimization_barrier((mpo_sites[0, 1], below[1]))
    terms = [h0, *below, *above]
    *parts, h1, h0, first = site(1, (*scalars, flat_rule(second_rule)), terms, near)
    below, above = moved(sector, h1, parts[:2], parts[2:])
    pair_rules, below[1] = lax.optimization_barrier((mpo_pair[0], below[1]))
    ket = sector + class_shift(channel_class)
    sectors = jnp.arange(NSEC, dtype=jnp.int32)
    width = jnp.arange(TILE, dtype=jnp.int32)
    count = jnp.where(ket[:, None] == sectors, live_rows[0, 1], 0).sum(-1)
    own = jnp.where(sector == sectors, live_rows[0, 1], 0).sum()
    keep = (width[:, None] < count[:, None, None]) & (width < own)
    parts = []
    passed = []
    for n, (lo, hi) in enumerate(CHUNKS):
        under = jnp.where(sector[0] % ND == 0, 0.0, below[n])
        second = jnp.where(keep[lo:hi], h0[lo:hi] + under + above[n], 0.0)
        second = jnp.where(region_sites[0] > 1, second, first[lo:hi])
        parts.append(second)
        passed.append(fetch(second, -1, "region"))

    environment = turned(parts)
    split = split_kets(sector, kets)
    scalars = (sector, region, channel_class, live_rows, *tables, flat_rule(pair_rules[0]), flat_rule(pair_rules[1]))
    images = pair(scalars, start, passed, split, [rights[u, d] for u in range(3) for d in range(3)])
    return environment[None, :, None], images[None, :, None]


def solution(mesh):
    in_specs = (
        P("region", None, "block", None, None),
        P("region", None, "block", None, None),
        P("region", None, None, "block", None, None),
        P("region", None, "block", None, None),
        P("region", None, None, None, None, None),
        P("region", None, None, None, None, None),
        P(),
        P("region", None, None),
        P("region"),
    )
    out_specs = (P("region", None, "block", None, None), P("region", None, "block", None, None))
    return jax.shard_map(shards, mesh=mesh, in_specs=in_specs, out_specs=out_specs, check_vma=False)
```
